128 devices in a mesh: expert: 64 (over x, y, z), dp: 2 (over core).
Axes of the slice: x: 4, y: 4, z: 4, core: 2. Of those that a mesh axis runs over, the one named last changes fastest.
Arguments:
- tokens: bfloat16 [12288, 4096], P(('expert', 'dp')), may hold values from -6 to 6
- w_gate: bfloat16 [128, 4096, 768], P(('expert', 'dp')), may hold values from -0.09375 to 0.09375
- w_up: bfloat16 [128, 4096, 768], P(('expert', 'dp')), may hold values from -0.09375 to 0.09375
- w_down: bfloat16 [128, 768, 4096], P(('expert', 'dp')), may hold values from -0.21875 to 0.21875
- route_ids: int32 [12288, 8], P(('expert', 'dp')), may hold values from 0 to 127, all different within a row
- route_gates: float32 [12288, 8], P(('expert', 'dp')), may hold values from 0.05 to 0.4
- hot_experts: int32 [1], replicated, may hold values from 0 to 127
Outputs:
- mixed: bfloat16 [12288, 4096], P(('expert', 'dp'))
The draws below stay inside these ranges and needn't reach their ends.
Inputs may be any that keep to these rules, and one draw needn't show every extreme that they name: `route_ids`: each row names 8 different experts.
All inputs are finite; a program needn't handle non-finite values.
Results may differ from the reference program's by a relative error of at most 0.007.
Values may be sent and summed in bfloat16 or wider, within the bound.
A program may use at most 192 MiB of HBM per device.

```python
import jax
import jax.numpy as jnp
from jax import lax

D = 4096
H = 768
TOP = 8
TOK_DEV = 96
CAP = 6
EXPERTS = 128
TOKENS = 12288
DEVICES = 128


def steps_of(own_key, shape, cuts, low, largest):
    factor_of = 1.0
    for dim, blocks in cuts:
        steps = jax.random.uniform(jax.random.fold_in(jax.random.fold_in(own_key, 6), dim), (blocks,), jnp.float32, low / len(cuts), largest / len(cuts))
        factor_of = factor_of * jnp.repeat(jnp.exp(steps), shape[dim] // blocks).reshape((-1,) + (1,) * (len(shape) - 1 - dim))
    return factor_of


def different_ones(own_key, rows, count, top, lift):
    sequence = jax.random.permutation(jax.random.fold_in(own_key, 1), count)
    favour = sequence
    for power in range(3):
        favour = favour * favour // count
    favour = favour * lift // count
    tickets = jax.random.randint(jax.random.fold_in(own_key, 2), (rows, count), 0, 4096) + favour
    holders = jax.random.permutation(jax.random.fold_in(own_key, 3), rows)[jnp.arange(count) % rows]
    tickets = jnp.where(jnp.arange(rows)[:, None] == holders[None, :], 1 << 14, tickets)
    score = tickets * count + jnp.arange(count)
    return lax.top_k(score.astype(jnp.int32), top)[1].astype(jnp.int32)


def gaussian(key, extent, scale, bound, split=(), kind=jnp.bfloat16):
    gain = steps_of(key, extent, split, -0.22, 0.18) if split else 1.0
    array = jax.random.normal(key, extent, jnp.float32) * scale * gain
    return jnp.minimum(jnp.maximum(array, -bound), bound).astype(kind)


def setup_inputs(seed: int = 0) -> dict:
    key_of = jax.random.split(jax.random.key(seed), 8)
    return {
        "tokens": gaussian(key_of[0], (TOKENS, D), 1.0, 6.0, ((0, 128),)),
        "w_gate": gaussian(key_of[1], (EXPERTS, D, H), D ** -0.5, 0.09375, ((0, 128),)),
        "w_up": gaussian(key_of[2], (EXPERTS, D, H), D ** -0.5, 0.09375, ((0, 128),)),
        "w_down": gaussian(key_of[3], (EXPERTS, H, D), H ** -0.5, 0.21875, ((0, 128),)),
        "route_ids": different_ones(key_of[4], TOKENS, EXPERTS, TOP, 1024),
        "route_gates": jnp.clip(0.05 + 0.35 * jax.random.uniform(key_of[5], (TOKENS, TOP), jnp.float32) ** steps_of(key_of[5], (TOKENS, TOP), ((0, 128),), -0.2, 0.2), 0.05, 0.4),
        "hot_experts": jax.random.randint(key_of[6], (1,), 0, EXPERTS).astype(jnp.int32),
    }


def expert_ffn(in_rows, gate_w, up_w, down_w):
    gate_val = jnp.dot(in_rows, gate_w, preferred_element_type=jnp.float32)
    up_val = jnp.dot(in_rows, up_w, preferred_element_type=jnp.float32)
    hidden = (jax.nn.silu(gate_val) * up_val).astype(jnp.bfloat16)
    return jnp.dot(hidden, down_w, preferred_element_type=jnp.float32).astype(jnp.bfloat16)


def reference(tokens, w_gate, w_up, w_down, route_ids, route_gates, hot_experts):
    hot_id = hot_experts[0]
    per_dev = route_ids.reshape(DEVICES, TOK_DEV * TOP)
    labels = jnp.arange(EXPERTS, dtype=jnp.int32)

    def ranks_of(ids_row):
        onehot = (ids_row[:, None] == labels[None, :]).astype(jnp.int32)
        return jnp.sum(onehot * (jnp.cumsum(onehot, axis=0) - 1), axis=1).astype(jnp.int32)

    rank_all = lax.map(ranks_of, per_dev).reshape(-1)
    flat_ids = route_ids.reshape(-1)
    is_kept = (flat_ids != hot_id) & (rank_all < CAP)
    token_idx = jnp.arange(TOKENS * TOP, dtype=jnp.int32) // TOP
    device_of = token_idx // TOK_DEV
    slot_of = jnp.where(is_kept, (flat_ids * DEVICES + device_of) * CAP + rank_all, EXPERTS * DEVICES * CAP).astype(jnp.int32)
    table = jnp.full((EXPERTS * DEVICES * CAP,), TOKENS, jnp.int32).at[slot_of].set(token_idx, mode="drop")
    weight_tab = jnp.zeros((EXPERTS * DEVICES * CAP,), jnp.float32).at[slot_of].set(route_gates.reshape(-1).astype(jnp.float32), mode="drop")
    table = table.reshape(EXPERTS, DEVICES * CAP)
    weight_tab = weight_tab.reshape(EXPERTS, DEVICES * CAP)
    padded = jnp.concatenate([tokens, jnp.zeros((1, D), tokens.dtype)], axis=0)

    def one_expert(combined, expert_id):
        in_rows = padded[table[expert_id]]
        result = expert_ffn(in_rows, w_gate[expert_id], w_up[expert_id], w_down[expert_id])
        weighted = result.astype(jnp.float32) * weight_tab[expert_id][:, None]
        return combined.at[table[expert_id]].add(weighted, mode="drop"), None

    combined, _ = lax.scan(one_expert, jnp.zeros((TOKENS, D), jnp.float32), jnp.arange(EXPERTS, dtype=jnp.int32))
    hot_out = expert_ffn(tokens, w_gate[hot_id], w_up[hot_id], w_down[hot_id])
    hot_weight = jnp.sum(jnp.where(route_ids == hot_id, route_gates, jnp.zeros_like(route_gates)), axis=1)
    combined = combined + hot_weight[:, None] * hot_out.astype(jnp.float32)
    return combined.astype(jnp.bfloat16)
```

```python
import jax
import jax.numpy as jnp
from jax import lax
from jax.sharding import PartitionSpec as P

CAP = 6


def expert_ffn(in_rows, gate_w, up_w, down_w):
    gate_val = jnp.dot(in_rows, gate_w, preferred_element_type=jnp.float32)
    up_val = jnp.dot(in_rows, up_w, preferred_element_type=jnp.float32)
    hidden = (jax.nn.silu(gate_val) * up_val).astype(jnp.bfloat16)
    return jnp.dot(hidden, down_w, preferred_element_type=jnp.float32).astype(jnp.bfloat16)


def on_device(tokens, w_gate, w_up, w_down, route_ids, route_gates, hot_experts):
    feat_width = tokens.shape[1]
    tok_rows = tokens.shape[0]
    top_k = route_ids.shape[1]
    n_dp = lax.axis_size("dp")
    experts = lax.axis_size("expert") * n_dp
    hot_id = hot_experts[0]
    me = lax.axis_index("expert") * n_dp + lax.axis_index("dp")
    own = (w_gate[0], w_up[0], w_down[0])

    with jax.named_scope("hot_weight_broadcast"):
        is_root = me == hot_id
        hot_w = tuple(
            lax.psum(jnp.where(is_root, w, jnp.zeros_like(w)), ("expert", "dp")) for w in own
        )

    with jax.named_scope("routing"):
        flat_ids = route_ids.reshape(-1)
        labels = lax.iota(jnp.int32, experts)
        onehot = (flat_ids[:, None] == labels[None, :]).astype(jnp.int32)
        rank_of = jnp.sum(onehot * (jnp.cumsum(onehot, axis=0) - 1), axis=1)
        is_kept = (flat_ids != hot_id) & (rank_of < CAP)
        slot_of = jnp.where(is_kept, flat_ids * CAP + rank_of, experts * CAP)
        slots = lax.iota(jnp.int32, experts * CAP)
        hit = slot_of[None, :] == slots[:, None]
        dispatch = jnp.any(hit.reshape(experts * CAP, tok_rows, top_k), axis=2)

    with jax.named_scope("dispatch"):
        outgoing = jnp.dot(
            dispatch.astype(tokens.dtype), tokens, preferred_element_type=jnp.float32
        ).astype(tokens.dtype)
        to_send = outgoing.reshape(experts, CAP * feat_width)
        arrived = lax.all_to_all(to_send, ("expert", "dp"), 0, 0, tiled=True)

    with jax.named_scope("expert_ffn"):
        results = expert_ffn(arrived.reshape(-1, feat_width), *own)

    with jax.named_scope("return"):
        come_back = lax.all_to_all(
            results.reshape(experts, CAP * feat_width), ("expert", "dp"), 0, 0, tiled=True
        )
        returned = come_back.reshape(experts * CAP, feat_width)

    with jax.named_scope("combine"):
        gate_flat = route_gates.reshape(-1)
        cold_weight = jnp.where(is_kept, gate_flat, jnp.zeros_like(gate_flat))
        weight_of_slot = jnp.where(hit, cold_weight[None, :], 0.0)
        combine = jnp.sum(weight_of_slot.reshape(experts * CAP, tok_rows, top_k), axis=2).T
        cold_sum = jnp.dot(
            combine,
            returned.astype(jnp.float32),
            precision=lax.Precision.HIGHEST,
            preferred_element_type=jnp.float32,
        )

    with jax.named_scope("hot_expert"):
        hot_out = expert_ffn(tokens, *hot_w)
        hot_weight = jnp.sum(
            jnp.where(route_ids == hot_id, route_gates, jnp.zeros_like(route_gates)), axis=1
        )
        combined = cold_sum + hot_weight[:, None] * hot_out.astype(jnp.float32)
    return combined.astype(jnp.bfloat16)


def solution(mesh):
    in_specs = (
        P(("expert", "dp"), None),
        P(("expert", "dp"), None, None),
        P(("expert", "dp"), None, None),
        P(("expert", "dp"), None, None),
        P(("expert", "dp"), None),
        P(("expert", "dp"), None),
        P(),
    )
    out_specs = P(("expert", "dp"), None)
    return jax.shard_map(
        on_device, mesh=mesh, in_specs=in_specs, out_specs=out_specs, check_vma=False
    )
```

```python
import functools
import jax
import jax.numpy as jnp
from jax import lax
from jax.sharding import PartitionSpec as P
from jax.experimental import pallas as pl
from jax.experimental.pallas import tpu as pltpu


CAP = 6
MESH = pl.DeviceIdType.MESH


def a2a_kernel(n_dp, x_ref, y_ref, send_sem, recv_sem, local_sem):
    n = x_ref.shape[0]
    me = lax.axis_index("expert") * n_dp + lax.axis_index("dp")

    def peer_copy(src, dst, slot, peer):
        return pltpu.make_async_remote_copy(
            src_ref=x_ref.at[src],
            dst_ref=y_ref.at[dst],
            send_sem=send_sem.at[slot],
            recv_sem=recv_sem.at[slot],
            device_id=(peer // n_dp, peer % n_dp),
            device_id_type=MESH,
        )

    local = pltpu.make_async_copy(x_ref.at[me], y_ref.at[me], local_sem)
    local.start()

    def start(k, carry):
        peer = lax.rem(me + k, n)
        pltpu.make_async_remote_copy(
            src_ref=x_ref.at[peer],
            dst_ref=y_ref.at[me],
            send_sem=send_sem.at[peer],
            recv_sem=recv_sem.at[me],
            device_id=(peer // n_dp, peer % n_dp),
            device_id_type=MESH,
        ).start()
        return carry

    lax.fori_loop(1, n, start, 0)

    def finish(k, carry):
        peer = lax.rem(me + k, n)
        peer_copy(peer, peer, peer, peer).wait_send()
        peer_copy(peer, peer, peer, peer).wait_recv()
        return carry

    lax.fori_loop(1, n, finish, 0)
    local.wait()


def all_to_all_slabs(x, n_dp):
    n = x.shape[0]
    return pl.pallas_call(
        functools.partial(a2a_kernel, n_dp),
        out_shape=jax.ShapeDtypeStruct(x.shape, x.dtype),
        in_specs=[pl.BlockSpec(memory_space=pl.ANY)],
        out_specs=pl.BlockSpec(memory_space=pl.ANY),
        scratch_shapes=[
            pltpu.SemaphoreType.DMA((n,)),
            pltpu.SemaphoreType.DMA((n,)),
            pltpu.SemaphoreType.DMA(()),
        ],
        compiler_params=pltpu.CompilerParams(has_side_effects=True),
    )(x)


def expert_ffn(in_rows, gate_w, up_w, down_w):
    gate_val = jnp.dot(in_rows, gate_w, preferred_element_type=jnp.float32)
    up_val = jnp.dot(in_rows, up_w, preferred_element_type=jnp.float32)
    hidden = (jax.nn.silu(gate_val) * up_val).astype(jnp.bfloat16)
    return jnp.dot(hidden, down_w, preferred_element_type=jnp.float32).astype(jnp.bfloat16)


def on_device(tokens, w_gate, w_up, w_down, route_ids, route_gates, hot_experts):
    feat_width = tokens.shape[1]
    tok_rows = tokens.shape[0]
    top_k = route_ids.shape[1]
    n_dp = lax.axis_size("dp")
    experts = lax.axis_size("expert") * n_dp
    hot_id = hot_experts[0]
    me = lax.axis_index("expert") * n_dp + lax.axis_index("dp")
    own = (w_gate[0], w_up[0], w_down[0])

    with jax.named_scope("hot_weight_broadcast"):
        is_root = me == hot_id
        hot_w = tuple(
            lax.psum(jnp.where(is_root, w, jnp.zeros_like(w)), ("expert", "dp")) for w in own
        )

    with jax.named_scope("routing"):
        flat_ids = route_ids.reshape(-1)
        labels = lax.iota(jnp.int32, experts)
        onehot = (flat_ids[:, None] == labels[None, :]).astype(jnp.int32)
        rank_of = jnp.sum(onehot * (jnp.cumsum(onehot, axis=0) - 1), axis=1)
        is_kept = (flat_ids != hot_id) & (rank_of < CAP)
        slot_of = jnp.where(is_kept, flat_ids * CAP + rank_of, experts * CAP)
        slots = lax.iota(jnp.int32, experts * CAP)
        hit = slot_of[None, :] == slots[:, None]
        dispatch = jnp.any(hit.reshape(experts * CAP, tok_rows, top_k), axis=2)

    with jax.named_scope("dispatch"):
        outgoing = jnp.dot(
            dispatch.astype(tokens.dtype), tokens, preferred_element_type=jnp.float32
        ).astype(tokens.dtype)
        arrived = all_to_all_slabs(outgoing.reshape(experts, CAP, feat_width), n_dp)

    with jax.named_scope("expert_ffn"):
        results = expert_ffn(arrived.reshape(-1, feat_width), *own)

    with jax.named_scope("return"):
        come_back = all_to_all_slabs(results.reshape(experts, CAP, feat_width), n_dp)
        returned = come_back.reshape(experts * CAP, feat_width)

    with jax.named_scope("combine"):
        gate_flat = route_gates.reshape(-1)
        cold_weight = jnp.where(is_kept, gate_flat, jnp.zeros_like(gate_flat))
        weight_of_slot = jnp.where(hit, cold_weight[None, :], 0.0)
        combine = jnp.sum(weight_of_slot.reshape(experts * CAP, tok_rows, top_k), axis=2).T
        cold_sum = jnp.dot(
            combine,
            returned.astype(jnp.float32),
            precision=lax.Precision.HIGHEST,
            preferred_element_type=jnp.float32,
        )

    with jax.named_scope("hot_expert"):
        hot_out = expert_ffn(tokens, *hot_w)
        hot_weight = jnp.sum(
            jnp.where(route_ids == hot_id, route_gates, jnp.zeros_like(route_gates)), axis=1
        )
        combined = cold_sum + hot_weight[:, None] * hot_out.astype(jnp.float32)
    return combined.astype(jnp.bfloat16)


def solution(mesh):
    in_specs = (
        P(("expert", "dp"), None),
        P(("expert", "dp"), None, None),
        P(("expert", "dp"), None, None),
        P(("expert", "dp"), None, None),
        P(("expert", "dp"), None),
        P(("expert", "dp"), None),
        P(),
    )
    out_specs = P(("expert", "dp"), None)
    return jax.shard_map(
        on_device, mesh=mesh, in_specs=in_specs, out_specs=out_specs, check_vma=False
    )
```

```python
import functools
import jax
import jax.numpy as jnp
from jax import lax
from jax.sharding import PartitionSpec as P
from jax.experimental import pallas as pl
from jax.experimental.pallas import tpu as pltpu


CAP = 6
MESH = pl.DeviceIdType.MESH


def a2a_kernel(n_dp, x_ref, y_ref, send_sem, recv_sem, local_sem):
    n = x_ref.shape[0]
    me = lax.axis_index("expert") * n_dp + lax.axis_index("dp")

    def peer_copy(src, dst, slot, peer):
        return pltpu.make_async_remote_copy(
            src_ref=x_ref.at[src],
            dst_ref=y_ref.at[dst],
            send_sem=send_sem.at[slot],
            recv_sem=recv_sem.at[slot],
            device_id=(peer // n_dp, peer % n_dp),
            device_id_type=MESH,
        )

    local = pltpu.make_async_copy(x_ref.at[me], y_ref.at[me], local_sem)
    local.start()

    def start(k, carry):
        peer = lax.rem(me + k, n)
        pltpu.make_async_remote_copy(
            src_ref=x_ref.at[peer],
            dst_ref=y_ref.at[me],
            send_sem=send_sem.at[peer],
            recv_sem=recv_sem.at[me],
            device_id=(peer // n_dp, peer % n_dp),
            device_id_type=MESH,
        ).start()
        return carry

    lax.fori_loop(1, n, start, 0)

    def finish(k, carry):
        peer = lax.rem(me + k, n)
        peer_copy(peer, peer, peer, peer).wait_send()
        peer_copy(peer, peer, peer, peer).wait_recv()
        return carry

    lax.fori_loop(1, n, finish, 0)
    local.wait()


def all_to_all_slabs(x, n_dp):
    n = x.shape[0]
    return pl.pallas_call(
        functools.partial(a2a_kernel, n_dp),
        out_shape=jax.ShapeDtypeStruct(x.shape, x.dtype),
        in_specs=[pl.BlockSpec(memory_space=pl.ANY)],
        out_specs=pl.BlockSpec(memory_space=pl.ANY),
        scratch_shapes=[
            pltpu.SemaphoreType.DMA((n,)),
            pltpu.SemaphoreType.DMA((n,)),
            pltpu.SemaphoreType.DMA(()),
        ],
        compiler_params=pltpu.CompilerParams(has_side_effects=True),
    )(x)


def expert_ffn(in_rows, gate_w, up_w, down_w):
    gate_val = jnp.dot(in_rows, gate_w, preferred_element_type=jnp.float32)
    up_val = jnp.dot(in_rows, up_w, preferred_element_type=jnp.float32)
    hidden = (jax.nn.silu(gate_val) * up_val).astype(jnp.bfloat16)
    return jnp.dot(hidden, down_w, preferred_element_type=jnp.float32).astype(jnp.bfloat16)


def on_device(tokens, w_gate, w_up, w_down, route_ids, route_gates, hot_experts):
    tok_rows = tokens.shape[0]
    top_k = route_ids.shape[1]
    n_dp = lax.axis_size("dp")
    experts = lax.axis_size("expert") * n_dp
    hot_id = hot_experts[0]
    me = lax.axis_index("expert") * n_dp + lax.axis_index("dp")
    own = (w_gate[0], w_up[0], w_down[0])

    with jax.named_scope("routing"):
        flat_ids = route_ids.reshape(-1)
        labels = lax.iota(jnp.int32, experts)
        onehot = (flat_ids[:, None] == labels[None, :]).astype(jnp.int32)
        rank_of = jnp.sum(onehot * (jnp.cumsum(onehot, axis=0) - 1), axis=1)
        is_kept = (flat_ids != hot_id) & (rank_of < CAP)
        slot_rank = lax.iota(jnp.int32, CAP)
        hit = (flat_ids[None, None, :] == labels[:, None, None]) & (
            rank_of[None, None, :] == slot_rank[None, :, None]
        ) & is_kept[None, None, :]
        dispatch = jnp.any(hit.reshape(experts, CAP, tok_rows, top_k), axis=3)

    with jax.named_scope("dispatch"):
        outgoing = jnp.einsum(
            "esp,pd->esd", dispatch.astype(tokens.dtype), tokens,
            preferred_element_type=jnp.float32,
        ).astype(tokens.dtype)
        arrived = lax.all_to_all(outgoing, ("expert", "dp"), 0, 0, tiled=True)

    with jax.named_scope("hot_weight_broadcast"):
        is_root = me == hot_id
        hot_w = tuple(
            lax.psum(jnp.where(is_root, w, jnp.zeros_like(w)), ("expert", "dp")) for w in own
        )

    with jax.named_scope("expert_ffn"):
        gate_val = jnp.einsum("esd,dh->esh", arrived, own[0], preferred_element_type=jnp.float32)
        up_val = jnp.einsum("esd,dh->esh", arrived, own[1], preferred_element_type=jnp.float32)
        hidden = (jax.nn.silu(gate_val) * up_val).astype(jnp.bfloat16)
        results = jnp.einsum(
            "esh,hd->esd", hidden, own[2], preferred_element_type=jnp.float32
        ).astype(jnp.bfloat16)

    with jax.named_scope("return"):
        returned = lax.all_to_all(results, ("expert", "dp"), 0, 0, tiled=True)

    with jax.named_scope("combine"):
        gate_flat = route_gates.reshape(-1)
        cold_weight = jnp.where(is_kept, gate_flat, jnp.zeros_like(gate_flat))
        weight_of_slot = jnp.where(hit, cold_weight[None, None, :], 0.0)
        combine = jnp.sum(weight_of_slot.reshape(experts, CAP, tok_rows, top_k), axis=3)
        cold_sum = jnp.einsum(
            "esp,esd->pd",
            combine,
            returned.astype(jnp.float32),
            precision=lax.Precision.HIGHEST,
            preferred_element_type=jnp.float32,
        )

    with jax.named_scope("hot_expert"):
        hot_out = expert_ffn(tokens, *hot_w)
        hot_weight = jnp.sum(
            jnp.where(route_ids == hot_id, route_gates, jnp.zeros_like(route_gates)), axis=1
        )
        combined = cold_sum + hot_weight[:, None] * hot_out.astype(jnp.float32)
    return combined.astype(jnp.bfloat16)


def solution(mesh):
    in_specs = (
        P(("expert", "dp"), None),
        P(("expert", "dp"), None, None),
        P(("expert", "dp"), None, None),
        P(("expert", "dp"), None, None),
        P(("expert", "dp"), None),
        P(("expert", "dp"), None),
        P(),
    )
    out_specs = P(("expert", "dp"), None)
    return jax.shard_map(
        on_device, mesh=mesh, in_specs=in_specs, out_specs=out_specs, check_vma=False
    )
```

```python
import functools
import jax
import jax.numpy as jnp
from jax import lax
from jax.sharding import PartitionSpec as P
from jax.experimental import pallas as pl
from jax.experimental.pallas import tpu as pltpu


CAP = 6
MESH = pl.DeviceIdType.MESH


def a2a_kernel(n_dp, x_ref, y_ref, send_sem, recv_sem, local_sem):
    n = x_ref.shape[0]
    me = lax.axis_index("expert") * n_dp + lax.axis_index("dp")

    def peer_copy(src, dst, slot, peer):
        return pltpu.make_async_remote_copy(
            src_ref=x_ref.at[src],
            dst_ref=y_ref.at[dst],
            send_sem=send_sem.at[slot],
            recv_sem=recv_sem.at[slot],
            device_id=(peer // n_dp, peer % n_dp),
            device_id_type=MESH,
        )

    local = pltpu.make_async_copy(x_ref.at[me], y_ref.at[me], local_sem)
    local.start()

    def start(k, carry):
        peer = lax.rem(me + k, n)
        pltpu.make_async_remote_copy(
            src_ref=x_ref.at[peer],
            dst_ref=y_ref.at[me],
            send_sem=send_sem.at[peer],
            recv_sem=recv_sem.at[me],
            device_id=(peer // n_dp, peer % n_dp),
            device_id_type=MESH,
        ).start()
        return carry

    lax.fori_loop(1, n, start, 0)

    def finish(k, carry):
        peer = lax.rem(me + k, n)
        peer_copy(peer, peer, peer, peer).wait_send()
        peer_copy(peer, peer, peer, peer).wait_recv()
        return carry

    lax.fori_loop(1, n, finish, 0)
    local.wait()


def all_to_all_slabs(x, n_dp):
    n = x.shape[0]
    return pl.pallas_call(
        functools.partial(a2a_kernel, n_dp),
        out_shape=jax.ShapeDtypeStruct(x.shape, x.dtype),
        in_specs=[pl.BlockSpec(memory_space=pl.ANY)],
        out_specs=pl.BlockSpec(memory_space=pl.ANY),
        scratch_shapes=[
            pltpu.SemaphoreType.DMA((n,)),
            pltpu.SemaphoreType.DMA((n,)),
            pltpu.SemaphoreType.DMA(()),
        ],
        compiler_params=pltpu.CompilerParams(has_side_effects=True),
    )(x)


def expert_ffn(in_rows, gate_w, up_w, down_w):
    gate_val = jnp.dot(in_rows, gate_w, preferred_element_type=jnp.float32)
    up_val = jnp.dot(in_rows, up_w, preferred_element_type=jnp.float32)
    hidden = (jax.nn.silu(gate_val) * up_val).astype(jnp.bfloat16)
    return jnp.dot(hidden, down_w, preferred_element_type=jnp.float32).astype(jnp.bfloat16)


def on_device(tokens, w_gate, w_up, w_down, route_ids, route_gates, hot_experts):
    tok_rows = tokens.shape[0]
    top_k = route_ids.shape[1]
    n_dp = lax.axis_size("dp")
    experts = lax.axis_size("expert") * n_dp
    hot_id = hot_experts[0]
    me = lax.axis_index("expert") * n_dp + lax.axis_index("dp")
    own = (w_gate[0], w_up[0], w_down[0])

    with jax.named_scope("routing"):
        flat_ids = route_ids.reshape(-1)
        labels = lax.iota(jnp.int32, experts)
        onehot = (flat_ids[:, None] == labels[None, :]).astype(jnp.int32)
        rank_of = jnp.sum(onehot * (jnp.cumsum(onehot, axis=0) - 1), axis=1)
        is_kept = (flat_ids != hot_id) & (rank_of < CAP)
        slot_rank = lax.iota(jnp.int32, CAP)
        hit = (flat_ids[None, None, :] == labels[:, None, None]) & (
            rank_of[None, None, :] == slot_rank[None, :, None]
        ) & is_kept[None, None, :]
        dispatch = jnp.any(hit.reshape(experts, CAP, tok_rows, top_k), axis=3)

    with jax.named_scope("dispatch"):
        outgoing = jnp.einsum(
            "esp,pd->esd", dispatch.astype(tokens.dtype), tokens,
            preferred_element_type=jnp.float32,
        ).astype(tokens.dtype)
        arrived = lax.all_to_all(outgoing, ("expert", "dp"), 0, 0, tiled=True)

    with jax.named_scope("hot_weight_broadcast"):
        core = lax.axis_index("dp")
        partner = me + 1 - 2 * core
        half = own[0].shape[1] // 2
        split_g = own[0].reshape(own[0].shape[0], 2, half)
        split_u = own[1].reshape(own[1].shape[0], 2, half)
        split_d = own[2].reshape(2, half, own[2].shape[1])
        mine = (
            jnp.where(core == 0, split_g[:, 0], split_g[:, 1]),
            jnp.where(core == 0, split_u[:, 0], split_u[:, 1]),
            jnp.where(core == 0, split_d[0], split_d[1]),
        )
        theirs = (
            jnp.where(core == 0, split_g[:, 1], split_g[:, 0]),
            jnp.where(core == 0, split_u[:, 1], split_u[:, 0]),
            jnp.where(core == 0, split_d[1], split_d[0]),
        )
        swap = [(0, 1), (1, 0)]
        from_partner = tuple(lax.ppermute(w, "dp", swap) for w in theirs)
        held = tuple(
            jnp.where(me == hot_id, a, jnp.where(partner == hot_id, b, jnp.zeros_like(a)))
            for a, b in zip(mine, from_partner)
        )
        hot_w = tuple(lax.psum(w, "expert") for w in held)

    with jax.named_scope("expert_ffn"):
        gate_val = jnp.einsum("esd,dh->esh", arrived, own[0], preferred_element_type=jnp.float32)
        up_val = jnp.einsum("esd,dh->esh", arrived, own[1], preferred_element_type=jnp.float32)
        hidden = (jax.nn.silu(gate_val) * up_val).astype(jnp.bfloat16)
        results = jnp.einsum(
            "esh,hd->esd", hidden, own[2], preferred_element_type=jnp.float32
        ).astype(jnp.bfloat16)

    with jax.named_scope("return"):
        returned = lax.all_to_all(results, ("expert", "dp"), 0, 0, tiled=True)

    with jax.named_scope("combine"):
        gate_flat = route_gates.reshape(-1)
        cold_weight = jnp.where(is_kept, gate_flat, jnp.zeros_like(gate_flat))
        weight_of_slot = jnp.where(hit, cold_weight[None, None, :], 0.0)
        combine = jnp.sum(weight_of_slot.reshape(experts, CAP, tok_rows, top_k), axis=3)
        cold_sum = jnp.einsum(
            "esp,esd->pd",
            combine,
            returned.astype(jnp.float32),
            precision=lax.Precision.HIGHEST,
            preferred_element_type=jnp.float32,
        )

    with jax.named_scope("hot_expert"):
        pair = jnp.concatenate([tokens, lax.ppermute(tokens, "dp", swap)], axis=0)
        gate_val = jnp.dot(pair, hot_w[0], preferred_element_type=jnp.float32)
        up_val = jnp.dot(pair, hot_w[1], preferred_element_type=jnp.float32)
        hidden = (jax.nn.silu(gate_val) * up_val).astype(jnp.bfloat16)
        partial = jnp.dot(hidden, hot_w[2], preferred_element_type=jnp.float32)
        hot_out = (
            partial[:tok_rows] + lax.ppermute(partial[tok_rows:], "dp", swap)
        ).astype(jnp.bfloat16)
        hot_weight = jnp.sum(
            jnp.where(route_ids == hot_id, route_gates, jnp.zeros_like(route_gates)), axis=1
        )
        combined = cold_sum + hot_weight[:, None] * hot_out.astype(jnp.float32)
    return combined.astype(jnp.bfloat16)


def solution(mesh):
    in_specs = (
        P(("expert", "dp"), None),
        P(("expert", "dp"), None, None),
        P(("expert", "dp"), None, None),
        P(("expert", "dp"), None, None),
        P(("expert", "dp"), None),
        P(("expert", "dp"), None),
        P(),
    )
    out_specs = P(("expert", "dp"), None)
    return jax.shard_map(
        on_device, mesh=mesh, in_specs=in_specs, out_specs=out_specs, check_vma=False
    )
```

```python
import functools
import jax
import jax.numpy as jnp
from jax import lax
from jax.sharding import PartitionSpec as P
from jax.experimental import pallas as pl
from jax.experimental.pallas import tpu as pltpu


CAP = 6
MESH = pl.DeviceIdType.MESH


def a2a_kernel(n_dp, x_ref, y_ref, send_sem, recv_sem, local_sem):
    n = x_ref.shape[0]
    me = lax.axis_index("expert") * n_dp + lax.axis_index("dp")

    def peer_copy(src, dst, slot, peer):
        return pltpu.make_async_remote_copy(
            src_ref=x_ref.at[src],
            dst_ref=y_ref.at[dst],
            send_sem=send_sem.at[slot],
            recv_sem=recv_sem.at[slot],
            device_id=(peer // n_dp, peer % n_dp),
            device_id_type=MESH,
        )

    local = pltpu.make_async_copy(x_ref.at[me], y_ref.at[me], local_sem)
    local.start()

    def start(k, carry):
        peer = lax.rem(me + k, n)
        pltpu.make_async_remote_copy(
            src_ref=x_ref.at[peer],
            dst_ref=y_ref.at[me],
            send_sem=send_sem.at[peer],
            recv_sem=recv_sem.at[me],
            device_id=(peer // n_dp, peer % n_dp),
            device_id_type=MESH,
        ).start()
        return carry

    lax.fori_loop(1, n, start, 0)

    def finish(k, carry):
        peer = lax.rem(me + k, n)
        peer_copy(peer, peer, peer, peer).wait_send()
        peer_copy(peer, peer, peer, peer).wait_recv()
        return carry

    lax.fori_loop(1, n, finish, 0)
    local.wait()


def all_to_all_slabs(x, n_dp):
    n = x.shape[0]
    return pl.pallas_call(
        functools.partial(a2a_kernel, n_dp),
        out_shape=jax.ShapeDtypeStruct(x.shape, x.dtype),
        in_specs=[pl.BlockSpec(memory_space=pl.ANY)],
        out_specs=pl.BlockSpec(memory_space=pl.ANY),
        scratch_shapes=[
            pltpu.SemaphoreType.DMA((n,)),
            pltpu.SemaphoreType.DMA((n,)),
            pltpu.SemaphoreType.DMA(()),
        ],
        compiler_params=pltpu.CompilerParams(has_side_effects=True),
    )(x)


def expert_ffn(in_rows, gate_w, up_w, down_w):
    gate_val = jnp.dot(in_rows, gate_w, preferred_element_type=jnp.float32)
    up_val = jnp.dot(in_rows, up_w, preferred_element_type=jnp.float32)
    hidden = (jax.nn.silu(gate_val) * up_val).astype(jnp.bfloat16)
    return jnp.dot(hidden, down_w, preferred_element_type=jnp.float32).astype(jnp.bfloat16)


def on_device(tokens, w_gate, w_up, w_down, route_ids, route_gates, hot_experts):
    tok_rows = tokens.shape[0]
    top_k = route_ids.shape[1]
    n_dp = lax.axis_size("dp")
    experts = lax.axis_size("expert") * n_dp
    hot_id = hot_experts[0]
    me = lax.axis_index("expert") * n_dp + lax.axis_index("dp")
    own = (w_gate[0], w_up[0], w_down[0])

    with jax.named_scope("hot_weight_broadcast"):
        core = lax.axis_index("dp")
        partner = me + 1 - 2 * core
        half = own[0].shape[1] // 2
        split_g = own[0].reshape(own[0].shape[0], 2, half)
        split_u = own[1].reshape(own[1].shape[0], 2, half)
        split_d = own[2].reshape(2, half, own[2].shape[1])
        mine = (
            jnp.where(core == 0, split_g[:, 0], split_g[:, 1]),
            jnp.where(core == 0, split_u[:, 0], split_u[:, 1]),
            jnp.where(core == 0, split_d[0], split_d[1]),
        )
        theirs = (
            jnp.where(core == 0, split_g[:, 1], split_g[:, 0]),
            jnp.where(core == 0, split_u[:, 1], split_u[:, 0]),
            jnp.where(core == 0, split_d[1], split_d[0]),
        )
        swap = [(0, 1), (1, 0)]
        from_partner = tuple(lax.ppermute(w, "dp", swap) for w in theirs)
        held = tuple(
            jnp.where(me == hot_id, a, jnp.where(partner == hot_id, b, jnp.zeros_like(a)))
            for a, b in zip(mine, from_partner)
        )
        held, tokens = lax.optimization_barrier((held, tokens))
        hot_w = tuple(lax.psum(w, "expert") for w in held)

    with jax.named_scope("routing"):
        flat_ids = route_ids.reshape(-1)
        labels = lax.iota(jnp.int32, experts)
        onehot = (flat_ids[:, None] == labels[None, :]).astype(jnp.int32)
        rank_of = jnp.sum(onehot * (jnp.cumsum(onehot, axis=0) - 1), axis=1)
        is_kept = (flat_ids != hot_id) & (rank_of < CAP)
        slot_rank = lax.iota(jnp.int32, CAP)
        hit = (flat_ids[None, None, :] == labels[:, None, None]) & (
            rank_of[None, None, :] == slot_rank[None, :, None]
        ) & is_kept[None, None, :]
        dispatch = jnp.any(hit.reshape(experts, CAP, tok_rows, top_k), axis=3)

    with jax.named_scope("dispatch"):
        outgoing = jnp.einsum(
            "esp,pd->esd", dispatch.astype(tokens.dtype), tokens,
            preferred_element_type=jnp.float32,
        ).astype(tokens.dtype)
        arrived = lax.all_to_all(outgoing, ("expert", "dp"), 0, 0, tiled=True)

    with jax.named_scope("expert_ffn"):
        gate_val = jnp.einsum("esd,dh->esh", arrived, own[0], preferred_element_type=jnp.float32)
        up_val = jnp.einsum("esd,dh->esh", arrived, own[1], preferred_element_type=jnp.float32)
        hidden = (jax.nn.silu(gate_val) * up_val).astype(jnp.bfloat16)
        results = jnp.einsum(
            "esh,hd->esd", hidden, own[2], preferred_element_type=jnp.float32
        ).astype(jnp.bfloat16)

    with jax.named_scope("return"):
        returned = lax.all_to_all(results, ("expert", "dp"), 0, 0, tiled=True)

    with jax.named_scope("combine"):
        gate_flat = route_gates.reshape(-1)
        cold_weight = jnp.where(is_kept, gate_flat, jnp.zeros_like(gate_flat))
        weight_of_slot = jnp.where(hit, cold_weight[None, None, :], 0.0)
        combine = jnp.sum(weight_of_slot.reshape(experts, CAP, tok_rows, top_k), axis=3)
        combine_hi = combine.astype(jnp.bfloat16)
        combine_lo = (combine - combine_hi.astype(jnp.float32)).astype(jnp.bfloat16)
        cold_sum = jnp.einsum(
            "esp,esd->pd", combine_hi, returned, preferred_element_type=jnp.float32
        ) + jnp.einsum("esp,esd->pd", combine_lo, returned, preferred_element_type=jnp.float32)

    with jax.named_scope("hot_expert"):
        pair = jnp.concatenate([tokens, lax.ppermute(tokens, "dp", swap)], axis=0)
        gate_val = jnp.dot(pair, hot_w[0], preferred_element_type=jnp.float32)
        up_val = jnp.dot(pair, hot_w[1], preferred_element_type=jnp.float32)
        hidden = (jax.nn.silu(gate_val) * up_val).astype(jnp.bfloat16)
        partial = jnp.dot(hidden, hot_w[2], preferred_element_type=jnp.float32)
        hot_out = (
            partial[:tok_rows] + lax.ppermute(partial[tok_rows:], "dp", swap)
        ).astype(jnp.bfloat16)
        hot_weight = jnp.sum(
            jnp.where(route_ids == hot_id, route_gates, jnp.zeros_like(route_gates)), axis=1
        )
        combined = cold_sum + hot_weight[:, None] * hot_out.astype(jnp.float32)
    return combined.astype(jnp.bfloat16)


def solution(mesh):
    in_specs = (
        P(("expert", "dp"), None),
        P(("expert", "dp"), None, None),
        P(("expert", "dp"), None, None),
        P(("expert", "dp"), None, None),
        P(("expert", "dp"), None),
        P(("expert", "dp"), None),
        P(),
    )
    out_specs = P(("expert", "dp"), None)
    return jax.shard_map(
        on_device, mesh=mesh, in_specs=in_specs, out_specs=out_specs, check_vma=False
    )
```

```python
import functools
import jax
import jax.numpy as jnp
from jax import lax
from jax.sharding import PartitionSpec as P
from jax.experimental import pallas as pl
from jax.experimental.pallas import tpu as pltpu


CAP = 6
MESH = pl.DeviceIdType.MESH


def a2a_kernel(n_dp, x_ref, y_ref, send_sem, recv_sem, local_sem):
    n = x_ref.shape[0]
    me = lax.axis_index("expert") * n_dp + lax.axis_index("dp")

    def peer_copy(src, dst, slot, peer):
        return pltpu.make_async_remote_copy(
            src_ref=x_ref.at[src],
            dst_ref=y_ref.at[dst],
            send_sem=send_sem.at[slot],
            recv_sem=recv_sem.at[slot],
            device_id=(peer // n_dp, peer % n_dp),
            device_id_type=MESH,
        )

    local = pltpu.make_async_copy(x_ref.at[me], y_ref.at[me], local_sem)
    local.start()

    def start(k, carry):
        peer = lax.rem(me + k, n)
        pltpu.make_async_remote_copy(
            src_ref=x_ref.at[peer],
            dst_ref=y_ref.at[me],
            send_sem=send_sem.at[peer],
            recv_sem=recv_sem.at[me],
            device_id=(peer // n_dp, peer % n_dp),
            device_id_type=MESH,
        ).start()
        return carry

    lax.fori_loop(1, n, start, 0)

    def finish(k, carry):
        peer = lax.rem(me + k, n)
        peer_copy(peer, peer, peer, peer).wait_send()
        peer_copy(peer, peer, peer, peer).wait_recv()
        return carry

    lax.fori_loop(1, n, finish, 0)
    local.wait()


def all_to_all_slabs(x, n_dp):
    n = x.shape[0]
    return pl.pallas_call(
        functools.partial(a2a_kernel, n_dp),
        out_shape=jax.ShapeDtypeStruct(x.shape, x.dtype),
        in_specs=[pl.BlockSpec(memory_space=pl.ANY)],
        out_specs=pl.BlockSpec(memory_space=pl.ANY),
        scratch_shapes=[
            pltpu.SemaphoreType.DMA((n,)),
            pltpu.SemaphoreType.DMA((n,)),
            pltpu.SemaphoreType.DMA(()),
        ],
        compiler_params=pltpu.CompilerParams(has_side_effects=True),
    )(x)


def expert_ffn(in_rows, gate_w, up_w, down_w):
    gate_val = jnp.dot(in_rows, gate_w, preferred_element_type=jnp.float32)
    up_val = jnp.dot(in_rows, up_w, preferred_element_type=jnp.float32)
    hidden = (jax.nn.silu(gate_val) * up_val).astype(jnp.bfloat16)
    return jnp.dot(hidden, down_w, preferred_element_type=jnp.float32).astype(jnp.bfloat16)


def on_device(tokens, w_gate, w_up, w_down, route_ids, route_gates, hot_experts):
    tok_rows = tokens.shape[0]
    top_k = route_ids.shape[1]
    n_dp = lax.axis_size("dp")
    experts = lax.axis_size("expert") * n_dp
    hot_id = hot_experts[0]
    me = lax.axis_index("expert") * n_dp + lax.axis_index("dp")
    own = (w_gate[0], w_up[0], w_down[0])

    with jax.named_scope("routing"):
        flat_ids = route_ids.reshape(-1)
        labels = lax.iota(jnp.int32, experts)
        onehot = (flat_ids[:, None] == labels[None, :]).astype(jnp.int32)
        rank_of = jnp.sum(onehot * (jnp.cumsum(onehot, axis=0) - 1), axis=1)
        is_kept = (flat_ids != hot_id) & (rank_of < CAP)
        slot_rank = lax.iota(jnp.int32, CAP)
        hit = (flat_ids[None, None, :] == labels[:, None, None]) & (
            rank_of[None, None, :] == slot_rank[None, :, None]
        ) & is_kept[None, None, :]
        dispatch = jnp.any(hit.reshape(experts, CAP, tok_rows, top_k), axis=3)

    with jax.named_scope("dispatch"):
        outgoing = jnp.einsum(
            "esp,pd->esd", dispatch.astype(tokens.dtype), tokens,
            preferred_element_type=jnp.float32,
        ).astype(tokens.dtype)
        arrived = lax.all_to_all(outgoing, ("expert", "dp"), 0, 0, tiled=True)

    with jax.named_scope("hot_weight_broadcast"):
        core = lax.axis_index("dp")
        partner = me + 1 - 2 * core
        half = own[0].shape[1] // 2
        split_g = own[0].reshape(own[0].shape[0], 2, half)
        split_u = own[1].reshape(own[1].shape[0], 2, half)
        split_d = own[2].reshape(2, half, own[2].shape[1])
        mine = (
            jnp.where(core == 0, split_g[:, 0], split_g[:, 1]),
            jnp.where(core == 0, split_u[:, 0], split_u[:, 1]),
            jnp.where(core == 0, split_d[0], split_d[1]),
        )
        theirs = (
            jnp.where(core == 0, split_g[:, 1], split_g[:, 0]),
            jnp.where(core == 0, split_u[:, 1], split_u[:, 0]),
            jnp.where(core == 0, split_d[1], split_d[0]),
        )
        swap = [(0, 1), (1, 0)]
        from_partner = tuple(lax.ppermute(w, "dp", swap) for w in theirs)
        held = tuple(
            jnp.where(me == hot_id, a, jnp.where(partner == hot_id, b, jnp.zeros_like(a)))
            for a, b in zip(mine, from_partner)
        )
        hot_w = tuple(lax.psum(w, "expert") for w in held)

    with jax.named_scope("expert_ffn"):
        gate_val = jnp.einsum("esd,dh->esh", arrived, own[0], preferred_element_type=jnp.float32)
        up_val = jnp.einsum("esd,dh->esh", arrived, own[1], preferred_element_type=jnp.float32)
        hidden = (jax.nn.silu(gate_val) * up_val).astype(jnp.bfloat16)
        results = jnp.einsum(
            "esh,hd->esd", hidden, own[2], preferred_element_type=jnp.float32
        ).astype(jnp.bfloat16)

    with jax.named_scope("return"):
        returned = lax.all_to_all(results, ("expert", "dp"), 0, 0, tiled=True)

    with jax.named_scope("combine"):
        gate_flat = route_gates.reshape(-1)
        cold_weight = jnp.where(is_kept, gate_flat, jnp.zeros_like(gate_flat))
        weight_of_slot = jnp.where(hit, cold_weight[None, None, :], 0.0)
        combine = jnp.sum(weight_of_slot.reshape(experts, CAP, tok_rows, top_k), axis=3)
        cold_sum = jnp.einsum(
            "esp,esd->pd",
            combine,
            returned.astype(jnp.float32),
            precision=lax.Precision.HIGHEST,
            preferred_element_type=jnp.float32,
        )

    with jax.named_scope("hot_expert"):
        pair = jnp.concatenate([tokens, lax.ppermute(tokens, "dp", swap)], axis=0)
        cold_sum, pair = lax.optimization_barrier((cold_sum, pair))
        gate_val = jnp.dot(pair, hot_w[0], preferred_element_type=jnp.float32)
        up_val = jnp.dot(pair, hot_w[1], preferred_element_type=jnp.float32)
        hidden = (jax.nn.silu(gate_val) * up_val).astype(jnp.bfloat16)
        partial = jnp.dot(hidden, hot_w[2], preferred_element_type=jnp.float32)
        hot_out = (
            partial[:tok_rows] + lax.ppermute(partial[tok_rows:], "dp", swap)
        ).astype(jnp.bfloat16)
        hot_weight = jnp.sum(
            jnp.where(route_ids == hot_id, route_gates, jnp.zeros_like(route_gates)), axis=1
        )
        combined = cold_sum + hot_weight[:, None] * hot_out.astype(jnp.float32)
    return combined.astype(jnp.bfloat16)


def solution(mesh):
    in_specs = (
        P(("expert", "dp"), None),
        P(("expert", "dp"), None, None),
        P(("expert", "dp"), None, None),
        P(("expert", "dp"), None, None),
        P(("expert", "dp"), None),
        P(("expert", "dp"), None),
        P(),
    )
    out_specs = P(("expert", "dp"), None)
    return jax.shard_map(
        on_device, mesh=mesh, in_specs=in_specs, out_specs=out_specs, check_vma=False
    )
```

```python
import functools
import jax
import jax.numpy as jnp
from jax import lax
from jax.sharding import PartitionSpec as P
from jax.experimental import pallas as pl
from jax.experimental.pallas import tpu as pltpu


CAP = 6
MESH = pl.DeviceIdType.MESH


def a2a_kernel(n_dp, x_ref, y_ref, send_sem, recv_sem, local_sem):
    n = x_ref.shape[0]
    me = lax.axis_index("expert") * n_dp + lax.axis_index("dp")

    def peer_copy(src, dst, slot, peer):
        return pltpu.make_async_remote_copy(
            src_ref=x_ref.at[src],
            dst_ref=y_ref.at[dst],
            send_sem=send_sem.at[slot],
            recv_sem=recv_sem.at[slot],
            device_id=(peer // n_dp, peer % n_dp),
            device_id_type=MESH,
        )

    local = pltpu.make_async_copy(x_ref.at[me], y_ref.at[me], local_sem)
    local.start()

    def start(k, carry):
        peer = lax.rem(me + k, n)
        pltpu.make_async_remote_copy(
            src_ref=x_ref.at[peer],
            dst_ref=y_ref.at[me],
            send_sem=send_sem.at[peer],
            recv_sem=recv_sem.at[me],
            device_id=(peer // n_dp, peer % n_dp),
            device_id_type=MESH,
        ).start()
        return carry

    lax.fori_loop(1, n, start, 0)

    def finish(k, carry):
        peer = lax.rem(me + k, n)
        peer_copy(peer, peer, peer, peer).wait_send()
        peer_copy(peer, peer, peer, peer).wait_recv()
        return carry

    lax.fori_loop(1, n, finish, 0)
    local.wait()


def all_to_all_slabs(x, n_dp):
    n = x.shape[0]
    return pl.pallas_call(
        functools.partial(a2a_kernel, n_dp),
        out_shape=jax.ShapeDtypeStruct(x.shape, x.dtype),
        in_specs=[pl.BlockSpec(memory_space=pl.ANY)],
        out_specs=pl.BlockSpec(memory_space=pl.ANY),
        scratch_shapes=[
            pltpu.SemaphoreType.DMA((n,)),
            pltpu.SemaphoreType.DMA((n,)),
            pltpu.SemaphoreType.DMA(()),
        ],
        compiler_params=pltpu.CompilerParams(has_side_effects=True),
    )(x)


def expert_ffn(in_rows, gate_w, up_w, down_w):
    gate_val = jnp.dot(in_rows, gate_w, preferred_element_type=jnp.float32)
    up_val = jnp.dot(in_rows, up_w, preferred_element_type=jnp.float32)
    hidden = (jax.nn.silu(gate_val) * up_val).astype(jnp.bfloat16)
    return jnp.dot(hidden, down_w, preferred_element_type=jnp.float32).astype(jnp.bfloat16)


def on_device(tokens, w_gate, w_up, w_down, route_ids, route_gates, hot_experts):
    tok_rows = tokens.shape[0]
    top_k = route_ids.shape[1]
    n_dp = lax.axis_size("dp")
    experts = lax.axis_size("expert") * n_dp
    hot_id = hot_experts[0]
    me = lax.axis_index("expert") * n_dp + lax.axis_index("dp")
    own = (w_gate[0], w_up[0], w_down[0])

    with jax.named_scope("routing"):
        flat_ids = route_ids.reshape(-1)
        labels = lax.iota(jnp.int32, experts)
        onehot = (flat_ids[:, None] == labels[None, :]).astype(jnp.int32)
        rank_of = jnp.sum(onehot * (jnp.cumsum(onehot, axis=0) - 1), axis=1)
        is_kept = (flat_ids != hot_id) & (rank_of < CAP)
        slot_rank = lax.iota(jnp.int32, CAP)
        hit = (flat_ids[None, None, :] == labels[:, None, None]) & (
            rank_of[None, None, :] == slot_rank[None, :, None]
        ) & is_kept[None, None, :]
        dispatch = jnp.any(hit.reshape(experts, CAP, tok_rows, top_k), axis=3)

    with jax.named_scope("dispatch"):
        outgoing = jnp.einsum(
            "esp,pd->esd", dispatch.astype(tokens.dtype), tokens,
            preferred_element_type=jnp.float32,
        ).astype(tokens.dtype)
        arrived = lax.all_to_all(outgoing, ("expert", "dp"), 0, 0, tiled=True)

    with jax.named_scope("hot_weight_broadcast"):
        core = lax.axis_index("dp")
        partner = me + 1 - 2 * core
        half = own[0].shape[1] // 2
        rows = own[0].shape[0] // 2
        split_g = own[0].reshape(2, rows, own[0].shape[1])
        split_u = own[1].reshape(2, rows, own[1].shape[1])
        split_d = own[2].reshape(2, half, own[2].shape[1])
        mine = (
            jnp.where(core == 0, split_g[0], split_g[1]),
            jnp.where(core == 0, split_u[0], split_u[1]),
            jnp.where(core == 0, split_d[0], split_d[1]),
        )
        theirs = (
            jnp.where(core == 0, split_g[1], split_g[0]),
            jnp.where(core == 0, split_u[1], split_u[0]),
            jnp.where(core == 0, split_d[1], split_d[0]),
        )
        swap = [(0, 1), (1, 0)]
        from_partner = tuple(lax.ppermute(w, "dp", swap) for w in theirs)
        held = tuple(
            jnp.where(me == hot_id, a, jnp.where(partner == hot_id, b, jnp.zeros_like(a)))
            for a, b in zip(mine, from_partner)
        )
        hot_w = tuple(lax.psum(w, "expert") for w in held)

    with jax.named_scope("expert_ffn"):
        gate_val = jnp.einsum("esd,dh->esh", arrived, own[0], preferred_element_type=jnp.float32)
        up_val = jnp.einsum("esd,dh->esh", arrived, own[1], preferred_element_type=jnp.float32)
        hidden = (jax.nn.silu(gate_val) * up_val).astype(jnp.bfloat16)
        results = jnp.einsum(
            "esh,hd->esd", hidden, own[2], preferred_element_type=jnp.float32
        ).astype(jnp.bfloat16)

    with jax.named_scope("return"):
        returned = lax.all_to_all(results, ("expert", "dp"), 0, 0, tiled=True)

    with jax.named_scope("combine"):
        gate_flat = route_gates.reshape(-1)
        cold_weight = jnp.where(is_kept, gate_flat, jnp.zeros_like(gate_flat))
        weight_of_slot = jnp.where(hit, cold_weight[None, None, :], 0.0)
        combine = jnp.sum(weight_of_slot.reshape(experts, CAP, tok_rows, top_k), axis=3)
        cold_sum = jnp.einsum(
            "esp,esd->pd",
            combine,
            returned.astype(jnp.float32),
            precision=lax.Precision.HIGHEST,
            preferred_element_type=jnp.float32,
        )

    with jax.named_scope("hot_expert"):
        other_tokens = lax.ppermute(tokens, "dp", swap)
        pair = jnp.where(
            core == 0,
            jnp.concatenate([tokens, other_tokens], axis=0),
            jnp.concatenate([other_tokens, tokens], axis=0),
        )
        cold_sum, pair = lax.optimization_barrier((cold_sum, pair))
        cols = pair.reshape(pair.shape[0], 2, rows)
        pair_part = jnp.where(core == 0, cols[:, 0], cols[:, 1])
        gate_part = jnp.dot(pair_part, hot_w[0], preferred_element_type=jnp.float32)
        up_part = jnp.dot(pair_part, hot_w[1], preferred_element_type=jnp.float32)
        both = jnp.stack([gate_part, up_part]).reshape(2, pair.shape[0], 2, half)
        keep_part = jnp.where(core == 0, both[:, :, 0], both[:, :, 1])
        send_part = jnp.where(core == 0, both[:, :, 1], both[:, :, 0])
        full = keep_part + lax.ppermute(send_part, "dp", swap)
        hidden = (jax.nn.silu(full[0]) * full[1]).astype(jnp.bfloat16)
        partial = jnp.dot(hidden, hot_w[2], preferred_element_type=jnp.float32)
        by_core = partial.reshape(2, tok_rows, partial.shape[1])
        own_rows = jnp.where(core == 0, by_core[0], by_core[1])
        other_rows = jnp.where(core == 0, by_core[1], by_core[0])
        hot_out = (own_rows + lax.ppermute(other_rows, "dp", swap)).astype(jnp.bfloat16)
        hot_weight = jnp.sum(
            jnp.where(route_ids == hot_id, route_gates, jnp.zeros_like(route_gates)), axis=1
        )
        combined = cold_sum + hot_weight[:, None] * hot_out.astype(jnp.float32)
    return combined.astype(jnp.bfloat16)


def solution(mesh):
    in_specs = (
        P(("expert", "dp"), None),
        P(("expert", "dp"), None, None),
        P(("expert", "dp"), None, None),
        P(("expert", "dp"), None, None),
        P(("expert", "dp"), None),
        P(("expert", "dp"), None),
        P(),
    )
    out_specs = P(("expert", "dp"), None)
    return jax.shard_map(
        on_device, mesh=mesh, in_specs=in_specs, out_specs=out_specs, check_vma=False
    )
```

```python
import functools
import jax
import jax.numpy as jnp
from jax import lax
from jax.sharding import PartitionSpec as P
from jax.experimental import pallas as pl
from jax.experimental.pallas import tpu as pltpu


CAP = 6
SLOTS = 8
MESH = pl.DeviceIdType.MESH


def a2a_kernel(n_dp, x_ref, y_ref, send_sem, recv_sem, local_sem):
    n = x_ref.shape[0]
    me = lax.axis_index("expert") * n_dp + lax.axis_index("dp")

    def peer_copy(src, dst, slot, peer):
        return pltpu.make_async_remote_copy(
            src_ref=x_ref.at[src],
            dst_ref=y_ref.at[dst],
            send_sem=send_sem.at[slot],
            recv_sem=recv_sem.at[slot],
            device_id=(peer // n_dp, peer % n_dp),
            device_id_type=MESH,
        )

    local = pltpu.make_async_copy(x_ref.at[me], y_ref.at[me], local_sem)
    local.start()

    def start(k, carry):
        peer = lax.rem(me + k, n)
        pltpu.make_async_remote_copy(
            src_ref=x_ref.at[peer],
            dst_ref=y_ref.at[me],
            send_sem=send_sem.at[peer],
            recv_sem=recv_sem.at[me],
            device_id=(peer // n_dp, peer % n_dp),
            device_id_type=MESH,
        ).start()
        return carry

    lax.fori_loop(1, n, start, 0)

    def finish(k, carry):
        peer = lax.rem(me + k, n)
        peer_copy(peer, peer, peer, peer).wait_send()
        peer_copy(peer, peer, peer, peer).wait_recv()
        return carry

    lax.fori_loop(1, n, finish, 0)
    local.wait()


def all_to_all_slabs(x, n_dp):
    n = x.shape[0]
    return pl.pallas_call(
        functools.partial(a2a_kernel, n_dp),
        out_shape=jax.ShapeDtypeStruct(x.shape, x.dtype),
        in_specs=[pl.BlockSpec(memory_space=pl.ANY)],
        out_specs=pl.BlockSpec(memory_space=pl.ANY),
        scratch_shapes=[
            pltpu.SemaphoreType.DMA((n,)),
            pltpu.SemaphoreType.DMA((n,)),
            pltpu.SemaphoreType.DMA(()),
        ],
        compiler_params=pltpu.CompilerParams(has_side_effects=True),
    )(x)


def expert_ffn(in_rows, gate_w, up_w, down_w):
    gate_val = jnp.dot(in_rows, gate_w, preferred_element_type=jnp.float32)
    up_val = jnp.dot(in_rows, up_w, preferred_element_type=jnp.float32)
    hidden = (jax.nn.silu(gate_val) * up_val).astype(jnp.bfloat16)
    return jnp.dot(hidden, down_w, preferred_element_type=jnp.float32).astype(jnp.bfloat16)


def on_device(tokens, w_gate, w_up, w_down, route_ids, route_gates, hot_experts):
    tok_rows = tokens.shape[0]
    top_k = route_ids.shape[1]
    n_dp = lax.axis_size("dp")
    experts = lax.axis_size("expert") * n_dp
    hot_id = hot_experts[0]
    me = lax.axis_index("expert") * n_dp + lax.axis_index("dp")
    own = (w_gate[0], w_up[0], w_down[0])

    with jax.named_scope("routing"):
        flat_ids = route_ids.reshape(-1)
        labels = lax.iota(jnp.int32, experts)
        onehot = (flat_ids[:, None] == labels[None, :]).astype(jnp.int32)
        rank_of = jnp.sum(onehot * (jnp.cumsum(onehot, axis=0) - 1), axis=1)
        is_kept = (flat_ids != hot_id) & (rank_of < CAP)
        slot_rank = lax.iota(jnp.int32, CAP)
        hit = (flat_ids[None, None, :] == labels[:, None, None]) & (
            rank_of[None, None, :] == slot_rank[None, :, None]
        ) & is_kept[None, None, :]
        dispatch = jnp.any(hit.reshape(experts, CAP, tok_rows, top_k), axis=3)

    with jax.named_scope("dispatch"):
        padded = jnp.pad(dispatch, ((0, 0), (0, SLOTS - CAP), (0, 0)))
        outgoing = jnp.dot(
            padded.reshape(experts * SLOTS, tok_rows).astype(tokens.dtype), tokens,
            preferred_element_type=jnp.float32,
        ).astype(tokens.dtype)
        arrived = lax.all_to_all(
            outgoing.reshape(experts, SLOTS, -1), ("expert", "dp"), 0, 0, tiled=True
        )

    with jax.named_scope("hot_weight_broadcast"):
        core = lax.axis_index("dp")
        partner = me + 1 - 2 * core
        half = own[0].shape[1] // 2
        rows = own[0].shape[0] // 2
        split_g = own[0].reshape(2, rows, own[0].shape[1])
        split_u = own[1].reshape(2, rows, own[1].shape[1])
        split_d = own[2].reshape(2, half, own[2].shape[1])
        mine = (
            jnp.where(core == 0, split_g[0], split_g[1]),
            jnp.where(core == 0, split_u[0], split_u[1]),
            jnp.where(core == 0, split_d[0], split_d[1]),
        )
        theirs = (
            jnp.where(core == 0, split_g[1], split_g[0]),
            jnp.where(core == 0, split_u[1], split_u[0]),
            jnp.where(core == 0, split_d[1], split_d[0]),
        )
        swap = [(0, 1), (1, 0)]
        from_partner = tuple(lax.ppermute(w, "dp", swap) for w in theirs)
        held = tuple(
            jnp.where(me == hot_id, a, jnp.where(partner == hot_id, b, jnp.zeros_like(a)))
            for a, b in zip(mine, from_partner)
        )
        hot_w = tuple(lax.psum(w, "expert") for w in held)

    with jax.named_scope("expert_ffn"):
        results = expert_ffn(arrived.reshape(experts * SLOTS, -1), *own)

    with jax.named_scope("return"):
        returned = lax.all_to_all(
            results.reshape(experts, SLOTS, -1), ("expert", "dp"), 0, 0, tiled=True
        ).reshape(experts * SLOTS, -1)

    with jax.named_scope("combine"):
        gate_flat = route_gates.reshape(-1)
        cold_weight = jnp.where(is_kept, gate_flat, jnp.zeros_like(gate_flat))
        weight_of_slot = jnp.where(hit, cold_weight[None, None, :], 0.0)
        combine = jnp.sum(weight_of_slot.reshape(experts, CAP, tok_rows, top_k), axis=3)
        combine = jnp.pad(combine, ((0, 0), (0, SLOTS - CAP), (0, 0)))
        cold_sum = jnp.einsum(
            "sp,sd->pd",
            combine.reshape(experts * SLOTS, tok_rows),
            returned.astype(jnp.float32),
            precision=lax.Precision.HIGHEST,
            preferred_element_type=jnp.float32,
        )

    with jax.named_scope("hot_expert"):
        other_tokens = lax.ppermute(tokens, "dp", swap)
        pair = jnp.where(
            core == 0,
            jnp.concatenate([tokens, other_tokens], axis=0),
            jnp.concatenate([other_tokens, tokens], axis=0),
        )
        cold_sum, pair = lax.optimization_barrier((cold_sum, pair))
        cols = pair.reshape(pair.shape[0], 2, rows)
        pair_part = jnp.where(core == 0, cols[:, 0], cols[:, 1])
        gate_part = jnp.dot(pair_part, hot_w[0], preferred_element_type=jnp.float32)
        up_part = jnp.dot(pair_part, hot_w[1], preferred_element_type=jnp.float32)
        both = jnp.stack([gate_part, up_part]).reshape(2, pair.shape[0], 2, half)
        keep_part = jnp.where(core == 0, both[:, :, 0], both[:, :, 1])
        send_part = jnp.where(core == 0, both[:, :, 1], both[:, :, 0])
        full = keep_part + lax.ppermute(send_part, "dp", swap)
        hidden = (jax.nn.silu(full[0]) * full[1]).astype(jnp.bfloat16)
        partial = jnp.dot(hidden, hot_w[2], preferred_element_type=jnp.float32)
        by_core = partial.reshape(2, tok_rows, partial.shape[1])
        own_rows = jnp.where(core == 0, by_core[0], by_core[1])
        other_rows = jnp.where(core == 0, by_core[1], by_core[0])
        hot_out = (own_rows + lax.ppermute(other_rows, "dp", swap)).astype(jnp.bfloat16)
        hot_weight = jnp.sum(
            jnp.where(route_ids == hot_id, route_gates, jnp.zeros_like(route_gates)), axis=1
        )
        combined = cold_sum + hot_weight[:, None] * hot_out.astype(jnp.float32)
    return combined.astype(jnp.bfloat16)


def solution(mesh):
    in_specs = (
        P(("expert", "dp"), None),
        P(("expert", "dp"), None, None),
        P(("expert", "dp"), None, None),
        P(("expert", "dp"), None, None),
        P(("expert", "dp"), None),
        P(("expert", "dp"), None),
        P(),
    )
    out_specs = P(("expert", "dp"), None)
    return jax.shard_map(
        on_device, mesh=mesh, in_specs=in_specs, out_specs=out_specs, check_vma=False
    )
```

```python
import functools
import jax
import jax.numpy as jnp
from jax import lax
from jax.sharding import PartitionSpec as P
from jax.experimental import pallas as pl
from jax.experimental.pallas import tpu as pltpu


CAP = 6
MESH = pl.DeviceIdType.MESH


def a2a_kernel(n_dp, x_ref, y_ref, send_sem, recv_sem, local_sem):
    n = x_ref.shape[0]
    me = lax.axis_index("expert") * n_dp + lax.axis_index("dp")

    def peer_copy(src, dst, slot, peer):
        return pltpu.make_async_remote_copy(
            src_ref=x_ref.at[src],
            dst_ref=y_ref.at[dst],
            send_sem=send_sem.at[slot],
            recv_sem=recv_sem.at[slot],
            device_id=(peer // n_dp, peer % n_dp),
            device_id_type=MESH,
        )

    local = pltpu.make_async_copy(x_ref.at[me], y_ref.at[me], local_sem)
    local.start()

    def start(k, carry):
        peer = lax.rem(me + k, n)
        pltpu.make_async_remote_copy(
            src_ref=x_ref.at[peer],
            dst_ref=y_ref.at[me],
            send_sem=send_sem.at[peer],
            recv_sem=recv_sem.at[me],
            device_id=(peer // n_dp, peer % n_dp),
            device_id_type=MESH,
        ).start()
        return carry

    lax.fori_loop(1, n, start, 0)

    def finish(k, carry):
        peer = lax.rem(me + k, n)
        peer_copy(peer, peer, peer, peer).wait_send()
        peer_copy(peer, peer, peer, peer).wait_recv()
        return carry

    lax.fori_loop(1, n, finish, 0)
    local.wait()


def all_to_all_slabs(x, n_dp):
    n = x.shape[0]
    return pl.pallas_call(
        functools.partial(a2a_kernel, n_dp),
        out_shape=jax.ShapeDtypeStruct(x.shape, x.dtype),
        in_specs=[pl.BlockSpec(memory_space=pl.ANY)],
        out_specs=pl.BlockSpec(memory_space=pl.ANY),
        scratch_shapes=[
            pltpu.SemaphoreType.DMA((n,)),
            pltpu.SemaphoreType.DMA((n,)),
            pltpu.SemaphoreType.DMA(()),
        ],
        compiler_params=pltpu.CompilerParams(has_side_effects=True),
    )(x)


def expert_ffn(in_rows, gate_w, up_w, down_w):
    gate_val = jnp.dot(in_rows, gate_w, preferred_element_type=jnp.float32)
    up_val = jnp.dot(in_rows, up_w, preferred_element_type=jnp.float32)
    hidden = (jax.nn.silu(gate_val) * up_val).astype(jnp.bfloat16)
    return jnp.dot(hidden, down_w, preferred_element_type=jnp.float32).astype(jnp.bfloat16)


def on_device(tokens, w_gate, w_up, w_down, route_ids, route_gates, hot_experts):
    tok_rows = tokens.shape[0]
    top_k = route_ids.shape[1]
    n_dp = lax.axis_size("dp")
    experts = lax.axis_size("expert") * n_dp
    hot_id = hot_experts[0]
    me = lax.axis_index("expert") * n_dp + lax.axis_index("dp")
    own = (w_gate[0], w_up[0], w_down[0])

    with jax.named_scope("routing"):
        flat_ids = route_ids.reshape(-1)
        labels = lax.iota(jnp.int32, experts)
        onehot = (flat_ids[:, None] == labels[None, :]).astype(jnp.int32)
        rank_of = jnp.sum(onehot * (jnp.cumsum(onehot, axis=0) - 1), axis=1)
        is_kept = (flat_ids != hot_id) & (rank_of < CAP)
        slot_rank = lax.iota(jnp.int32, CAP)
        hit = (flat_ids[None, None, :] == labels[:, None, None]) & (
            rank_of[None, None, :] == slot_rank[None, :, None]
        ) & is_kept[None, None, :]
        dispatch = jnp.any(hit.reshape(experts, CAP, tok_rows, top_k), axis=3)

    with jax.named_scope("dispatch"):
        outgoing = jnp.einsum(
            "esp,pd->esd", dispatch.astype(tokens.dtype), tokens,
            preferred_element_type=jnp.float32,
        ).astype(tokens.dtype)
        arrived = lax.all_to_all(outgoing, ("expert", "dp"), 0, 0, tiled=True)

    with jax.named_scope("hot_weight_broadcast"):
        core = lax.axis_index("dp")
        partner = me + 1 - 2 * core
        half = own[0].shape[1] // 2
        rows = own[0].shape[0] // 2
        split_g = own[0].reshape(2, rows, own[0].shape[1])
        split_u = own[1].reshape(2, rows, own[1].shape[1])
        split_d = own[2].reshape(2, half, own[2].shape[1])
        mine = (
            jnp.where(core == 0, split_g[0], split_g[1]),
            jnp.where(core == 0, split_u[0], split_u[1]),
            jnp.where(core == 0, split_d[0], split_d[1]),
        )
        theirs = (
            jnp.where(core == 0, split_g[1], split_g[0]),
            jnp.where(core == 0, split_u[1], split_u[0]),
            jnp.where(core == 0, split_d[1], split_d[0]),
        )
        swap = [(0, 1), (1, 0)]
        from_partner = tuple(lax.ppermute(w, "dp", swap) for w in theirs)
        held = tuple(
            jnp.where(me == hot_id, a, jnp.where(partner == hot_id, b, jnp.zeros_like(a)))
            for a, b in zip(mine, from_partner)
        )
        held = lax.optimization_barrier(held)
        hot_w = lax.optimization_barrier(tuple(lax.psum(w, "expert") for w in held))

    with jax.named_scope("expert_ffn"):
        gate_val = jnp.einsum("esd,dh->esh", arrived, own[0], preferred_element_type=jnp.float32)
        up_val = jnp.einsum("esd,dh->esh", arrived, own[1], preferred_element_type=jnp.float32)
        hidden = (jax.nn.silu(gate_val) * up_val).astype(jnp.bfloat16)
        results = jnp.einsum(
            "esh,hd->esd", hidden, own[2], preferred_element_type=jnp.float32
        ).astype(jnp.bfloat16)

    with jax.named_scope("return"):
        returned = lax.all_to_all(results, ("expert", "dp"), 0, 0, tiled=True)

    with jax.named_scope("combine"):
        gate_flat = route_gates.reshape(-1)
        cold_weight = jnp.where(is_kept, gate_flat, jnp.zeros_like(gate_flat))
        weight_of_slot = jnp.where(hit, cold_weight[None, None, :], 0.0)
        combine = jnp.sum(weight_of_slot.reshape(experts, CAP, tok_rows, top_k), axis=3)
        cold_sum = jnp.einsum(
            "esp,esd->pd",
            combine,
            returned.astype(jnp.float32),
            precision=lax.Precision.HIGHEST,
            preferred_element_type=jnp.float32,
        )

    with jax.named_scope("hot_expert"):
        other_tokens = lax.ppermute(tokens, "dp", swap)
        pair = jnp.where(
            core == 0,
            jnp.concatenate([tokens, other_tokens], axis=0),
            jnp.concatenate([other_tokens, tokens], axis=0),
        )
        cold_sum, pair = lax.optimization_barrier((cold_sum, pair))
        cols = pair.reshape(pair.shape[0], 2, rows)
        pair_part = jnp.where(core == 0, cols[:, 0], cols[:, 1])
        gate_part = jnp.dot(pair_part, hot_w[0], preferred_element_type=jnp.float32)
        up_part = jnp.dot(pair_part, hot_w[1], preferred_element_type=jnp.float32)
        both = jnp.stack([gate_part, up_part]).reshape(2, pair.shape[0], 2, half)
        keep_part = jnp.where(core == 0, both[:, :, 0], both[:, :, 1])
        send_part = jnp.where(core == 0, both[:, :, 1], both[:, :, 0])
        full = keep_part + lax.ppermute(send_part, "dp", swap)
        hidden = (jax.nn.silu(full[0]) * full[1]).astype(jnp.bfloat16)
        partial = jnp.dot(hidden, hot_w[2], preferred_element_type=jnp.float32)
        by_core = partial.reshape(2, tok_rows, partial.shape[1])
        own_rows = jnp.where(core == 0, by_core[0], by_core[1])
        other_rows = jnp.where(core == 0, by_core[1], by_core[0])
        hot_out = (own_rows + lax.ppermute(other_rows, "dp", swap)).astype(jnp.bfloat16)
        hot_weight = jnp.sum(
            jnp.where(route_ids == hot_id, route_gates, jnp.zeros_like(route_gates)), axis=1
        )
        combined = cold_sum + hot_weight[:, None] * hot_out.astype(jnp.float32)
    return combined.astype(jnp.bfloat16)


def solution(mesh):
    in_specs = (
        P(("expert", "dp"), None),
        P(("expert", "dp"), None, None),
        P(("expert", "dp"), None, None),
        P(("expert", "dp"), None, None),
        P(("expert", "dp"), None),
        P(("expert", "dp"), None),
        P(),
    )
    out_specs = P(("expert", "dp"), None)
    return jax.shard_map(
        on_device, mesh=mesh, in_specs=in_specs, out_specs=out_specs, check_vma=False
    )
```

```python
import functools
import jax
import jax.numpy as jnp
from jax import lax
from jax.sharding import PartitionSpec as P
from jax.experimental import pallas as pl
from jax.experimental.pallas import tpu as pltpu


CAP = 6
MESH = pl.DeviceIdType.MESH


def a2a_kernel(n_dp, x_ref, y_ref, send_sem, recv_sem, local_sem):
    n = x_ref.shape[0]
    me = lax.axis_index("expert") * n_dp + lax.axis_index("dp")

    def peer_copy(src, dst, slot, peer):
        return pltpu.make_async_remote_copy(
            src_ref=x_ref.at[src],
            dst_ref=y_ref.at[dst],
            send_sem=send_sem.at[slot],
            recv_sem=recv_sem.at[slot],
            device_id=(peer // n_dp, peer % n_dp),
            device_id_type=MESH,
        )

    local = pltpu.make_async_copy(x_ref.at[me], y_ref.at[me], local_sem)
    local.start()

    def start(k, carry):
        peer = lax.rem(me + k, n)
        pltpu.make_async_remote_copy(
            src_ref=x_ref.at[peer],
            dst_ref=y_ref.at[me],
            send_sem=send_sem.at[peer],
            recv_sem=recv_sem.at[me],
            device_id=(peer // n_dp, peer % n_dp),
            device_id_type=MESH,
        ).start()
        return carry

    lax.fori_loop(1, n, start, 0)

    def finish(k, carry):
        peer = lax.rem(me + k, n)
        peer_copy(peer, peer, peer, peer).wait_send()
        peer_copy(peer, peer, peer, peer).wait_recv()
        return carry

    lax.fori_loop(1, n, finish, 0)
    local.wait()


def all_to_all_slabs(x, n_dp):
    n = x.shape[0]
    return pl.pallas_call(
        functools.partial(a2a_kernel, n_dp),
        out_shape=jax.ShapeDtypeStruct(x.shape, x.dtype),
        in_specs=[pl.BlockSpec(memory_space=pl.ANY)],
        out_specs=pl.BlockSpec(memory_space=pl.ANY),
        scratch_shapes=[
            pltpu.SemaphoreType.DMA((n,)),
            pltpu.SemaphoreType.DMA((n,)),
            pltpu.SemaphoreType.DMA(()),
        ],
        compiler_params=pltpu.CompilerParams(has_side_effects=True),
    )(x)


def expert_ffn(in_rows, gate_w, up_w, down_w):
    gate_val = jnp.dot(in_rows, gate_w, preferred_element_type=jnp.float32)
    up_val = jnp.dot(in_rows, up_w, preferred_element_type=jnp.float32)
    hidden = (jax.nn.silu(gate_val) * up_val).astype(jnp.bfloat16)
    return jnp.dot(hidden, down_w, preferred_element_type=jnp.float32).astype(jnp.bfloat16)


def on_device(tokens, w_gate, w_up, w_down, route_ids, route_gates, hot_experts):
    tok_rows = tokens.shape[0]
    top_k = route_ids.shape[1]
    n_dp = lax.axis_size("dp")
    experts = lax.axis_size("expert") * n_dp
    hot_id = hot_experts[0]
    me = lax.axis_index("expert") * n_dp + lax.axis_index("dp")
    own = (w_gate[0], w_up[0], w_down[0])

    with jax.named_scope("routing"):
        flat_ids = route_ids.reshape(-1)
        labels = lax.iota(jnp.int32, experts)
        onehot = (flat_ids[:, None] == labels[None, :]).astype(jnp.int32)
        rank_of = jnp.sum(onehot * (jnp.cumsum(onehot, axis=0) - 1), axis=1)
        is_kept = (flat_ids != hot_id) & (rank_of < CAP)
        slot_rank = lax.iota(jnp.int32, CAP)
        hit = (flat_ids[None, None, :] == labels[:, None, None]) & (
            rank_of[None, None, :] == slot_rank[None, :, None]
        ) & is_kept[None, None, :]
        dispatch = jnp.any(hit.reshape(experts, CAP, tok_rows, top_k), axis=3)

    with jax.named_scope("dispatch"):
        outgoing = jnp.einsum(
            "esp,pd->esd", dispatch.astype(tokens.dtype), tokens,
            preferred_element_type=jnp.float32,
        ).astype(tokens.dtype)
        arrived = lax.all_to_all(outgoing, ("expert", "dp"), 0, 0, tiled=True)

    with jax.named_scope("hot_weight_broadcast"):
        core = lax.axis_index("dp")
        partner = me + 1 - 2 * core
        half = own[0].shape[1] // 2
        rows = own[0].shape[0] // 2
        split_g = own[0].reshape(2, rows, own[0].shape[1])
        split_u = own[1].reshape(2, rows, own[1].shape[1])
        split_d = own[2].reshape(2, half, own[2].shape[1])
        mine = (
            jnp.where(core == 0, split_g[0], split_g[1]),
            jnp.where(core == 0, split_u[0], split_u[1]),
            jnp.where(core == 0, split_d[0], split_d[1]),
        )
        theirs = (
            jnp.where(core == 0, split_g[1], split_g[0]),
            jnp.where(core == 0, split_u[1], split_u[0]),
            jnp.where(core == 0, split_d[1], split_d[0]),
        )
        swap = [(0, 1), (1, 0)]
        from_partner = tuple(lax.ppermute(w, "dp", swap) for w in theirs)
        held = tuple(
            jnp.where(me == hot_id, a, jnp.where(partner == hot_id, b, jnp.zeros_like(a)))
            for a, b in zip(mine, from_partner)
        )
        hot_w = tuple(lax.psum(w, "expert") for w in held)

    with jax.named_scope("expert_ffn"):
        results = expert_ffn(arrived.reshape(experts * CAP, -1), *own).reshape(arrived.shape)

    with jax.named_scope("return"):
        returned = lax.all_to_all(results, ("expert", "dp"), 0, 0, tiled=True)

    with jax.named_scope("combine"):
        gate_flat = route_gates.reshape(-1)
        cold_weight = jnp.where(is_kept, gate_flat, jnp.zeros_like(gate_flat))
        weight_of_slot = jnp.where(hit, cold_weight[None, None, :], 0.0)
        combine = jnp.sum(weight_of_slot.reshape(experts, CAP, tok_rows, top_k), axis=3)
        cold_sum = jnp.einsum(
            "esp,esd->pd",
            combine,
            returned.astype(jnp.float32),
            precision=lax.Precision.HIGHEST,
            preferred_element_type=jnp.float32,
        )

    with jax.named_scope("hot_expert"):
        other_tokens = lax.ppermute(tokens, "dp", swap)
        pair = jnp.where(
            core == 0,
            jnp.concatenate([tokens, other_tokens], axis=0),
            jnp.concatenate([other_tokens, tokens], axis=0),
        )
        cold_sum, pair = lax.optimization_barrier((cold_sum, pair))
        cols = pair.reshape(pair.shape[0], 2, rows)
        pair_part = jnp.where(core == 0, cols[:, 0], cols[:, 1])
        gate_part = jnp.dot(pair_part, hot_w[0], preferred_element_type=jnp.float32)
        up_part = jnp.dot(pair_part, hot_w[1], preferred_element_type=jnp.float32)
        both = jnp.stack([gate_part, up_part]).reshape(2, pair.shape[0], 2, half)
        keep_part = jnp.where(core == 0, both[:, :, 0], both[:, :, 1])
        send_part = jnp.where(core == 0, both[:, :, 1], both[:, :, 0])
        full = keep_part + lax.ppermute(send_part, "dp", swap)
        hidden = (jax.nn.silu(full[0]) * full[1]).astype(jnp.bfloat16)
        partial = jnp.dot(hidden, hot_w[2], preferred_element_type=jnp.float32)
        by_core = partial.reshape(2, tok_rows, partial.shape[1])
        own_rows = jnp.where(core == 0, by_core[0], by_core[1])
        other_rows = jnp.where(core == 0, by_core[1], by_core[0])
        hot_out = (own_rows + lax.ppermute(other_rows, "dp", swap)).astype(jnp.bfloat16)
        hot_weight = jnp.sum(
            jnp.where(route_ids == hot_id, route_gates, jnp.zeros_like(route_gates)), axis=1
        )
        combined = cold_sum + hot_weight[:, None] * hot_out.astype(jnp.float32)
    return combined.astype(jnp.bfloat16)


def solution(mesh):
    in_specs = (
        P(("expert", "dp"), None),
        P(("expert", "dp"), None, None),
        P(("expert", "dp"), None, None),
        P(("expert", "dp"), None, None),
        P(("expert", "dp"), None),
        P(("expert", "dp"), None),
        P(),
    )
    out_specs = P(("expert", "dp"), None)
    return jax.shard_map(
        on_device, mesh=mesh, in_specs=in_specs, out_specs=out_specs, check_vma=False
    )
```

```python
import functools
import jax
import jax.numpy as jnp
from jax import lax
from jax.sharding import PartitionSpec as P
from jax.experimental import pallas as pl
from jax.experimental.pallas import tpu as pltpu


CAP = 6
MESH = pl.DeviceIdType.MESH


def a2a_kernel(n_dp, x_ref, y_ref, send_sem, recv_sem, local_sem):
    n = x_ref.shape[0]
    me = lax.axis_index("expert") * n_dp + lax.axis_index("dp")

    def peer_copy(src, dst, slot, peer):
        return pltpu.make_async_remote_copy(
            src_ref=x_ref.at[src],
            dst_ref=y_ref.at[dst],
            send_sem=send_sem.at[slot],
            recv_sem=recv_sem.at[slot],
            device_id=(peer // n_dp, peer % n_dp),
            device_id_type=MESH,
        )

    local = pltpu.make_async_copy(x_ref.at[me], y_ref.at[me], local_sem)
    local.start()

    def start(k, carry):
        peer = lax.rem(me + k, n)
        pltpu.make_async_remote_copy(
            src_ref=x_ref.at[peer],
            dst_ref=y_ref.at[me],
            send_sem=send_sem.at[peer],
            recv_sem=recv_sem.at[me],
            device_id=(peer // n_dp, peer % n_dp),
            device_id_type=MESH,
        ).start()
        return carry

    lax.fori_loop(1, n, start, 0)

    def finish(k, carry):
        peer = lax.rem(me + k, n)
        peer_copy(peer, peer, peer, peer).wait_send()
        peer_copy(peer, peer, peer, peer).wait_recv()
        return carry

    lax.fori_loop(1, n, finish, 0)
    local.wait()


def all_to_all_slabs(x, n_dp):
    n = x.shape[0]
    return pl.pallas_call(
        functools.partial(a2a_kernel, n_dp),
        out_shape=jax.ShapeDtypeStruct(x.shape, x.dtype),
        in_specs=[pl.BlockSpec(memory_space=pl.ANY)],
        out_specs=pl.BlockSpec(memory_space=pl.ANY),
        scratch_shapes=[
            pltpu.SemaphoreType.DMA((n,)),
            pltpu.SemaphoreType.DMA((n,)),
            pltpu.SemaphoreType.DMA(()),
        ],
        compiler_params=pltpu.CompilerParams(has_side_effects=True),
    )(x)


def expert_ffn(in_rows, gate_w, up_w, down_w):
    gate_val = jnp.dot(in_rows, gate_w, preferred_element_type=jnp.float32)
    up_val = jnp.dot(in_rows, up_w, preferred_element_type=jnp.float32)
    hidden = (jax.nn.silu(gate_val) * up_val).astype(jnp.bfloat16)
    return jnp.dot(hidden, down_w, preferred_element_type=jnp.float32).astype(jnp.bfloat16)


def on_device(tokens, w_gate, w_up, w_down, route_ids, route_gates, hot_experts):
    tok_rows = tokens.shape[0]
    top_k = route_ids.shape[1]
    n_dp = lax.axis_size("dp")
    experts = lax.axis_size("expert") * n_dp
    hot_id = hot_experts[0]
    me = lax.axis_index("expert") * n_dp + lax.axis_index("dp")
    own = (w_gate[0], w_up[0], w_down[0])

    with jax.named_scope("routing"):
        flat_ids = route_ids.reshape(-1)
        labels = lax.iota(jnp.int32, experts)
        onehot = (flat_ids[:, None] == labels[None, :]).astype(jnp.int32)
        rank_of = jnp.sum(onehot * (jnp.cumsum(onehot, axis=0) - 1), axis=1)
        is_kept = (flat_ids != hot_id) & (rank_of < CAP)
        slot_rank = lax.iota(jnp.int32, CAP)
        hit = (flat_ids[None, None, :] == labels[:, None, None]) & (
            rank_of[None, None, :] == slot_rank[None, :, None]
        ) & is_kept[None, None, :]
        dispatch = jnp.any(hit.reshape(experts, CAP, tok_rows, top_k), axis=3)

    with jax.named_scope("dispatch"):
        outgoing = jnp.dot(
            dispatch.reshape(experts * CAP, tok_rows).astype(tokens.dtype), tokens,
            preferred_element_type=jnp.float32,
        ).astype(tokens.dtype).reshape(experts, CAP, -1)
        arrived = lax.all_to_all(outgoing, ("expert", "dp"), 0, 0, tiled=True)

    with jax.named_scope("hot_weight_broadcast"):
        core = lax.axis_index("dp")
        partner = me + 1 - 2 * core
        half = own[0].shape[1] // 2
        rows = own[0].shape[0] // 2
        split_g = own[0].reshape(2, rows, own[0].shape[1])
        split_u = own[1].reshape(2, rows, own[1].shape[1])
        split_d = own[2].reshape(2, half, own[2].shape[1])
        mine = (
            jnp.where(core == 0, split_g[0], split_g[1]),
            jnp.where(core == 0, split_u[0], split_u[1]),
            jnp.where(core == 0, split_d[0], split_d[1]),
        )
        theirs = (
            jnp.where(core == 0, split_g[1], split_g[0]),
            jnp.where(core == 0, split_u[1], split_u[0]),
            jnp.where(core == 0, split_d[1], split_d[0]),
        )
        swap = [(0, 1), (1, 0)]
        from_partner = tuple(lax.ppermute(w, "dp", swap) for w in theirs)
        held = tuple(
            jnp.where(me == hot_id, a, jnp.where(partner == hot_id, b, jnp.zeros_like(a)))
            for a, b in zip(mine, from_partner)
        )
        hot_w = tuple(lax.psum(w, "expert") for w in held)

    with jax.named_scope("expert_ffn"):
        results = expert_ffn(arrived.reshape(experts * CAP, -1), *own).reshape(arrived.shape)

    with jax.named_scope("return"):
        returned = lax.all_to_all(results, ("expert", "dp"), 0, 0, tiled=True)

    with jax.named_scope("combine"):
        gate_flat = route_gates.reshape(-1)
        cold_weight = jnp.where(is_kept, gate_flat, jnp.zeros_like(gate_flat))
        weight_of_slot = jnp.where(hit, cold_weight[None, None, :], 0.0)
        combine = jnp.sum(weight_of_slot.reshape(experts, CAP, tok_rows, top_k), axis=3)
        cold_sum = jnp.einsum(
            "esp,esd->pd",
            combine,
            returned.astype(jnp.float32),
            precision=lax.Precision.HIGHEST,
            preferred_element_type=jnp.float32,
        )

    with jax.named_scope("hot_expert"):
        other_tokens = lax.ppermute(tokens, "dp", swap)
        pair = jnp.where(
            core == 0,
            jnp.concatenate([tokens, other_tokens], axis=0),
            jnp.concatenate([other_tokens, tokens], axis=0),
        )
        cold_sum, pair = lax.optimization_barrier((cold_sum, pair))
        cols = pair.reshape(pair.shape[0], 2, rows)
        pair_part = jnp.where(core == 0, cols[:, 0], cols[:, 1])
        gate_part = jnp.dot(pair_part, hot_w[0], preferred_element_type=jnp.float32)
        up_part = jnp.dot(pair_part, hot_w[1], preferred_element_type=jnp.float32)
        both = jnp.stack([gate_part, up_part]).reshape(2, pair.shape[0], 2, half)
        keep_part = jnp.where(core == 0, both[:, :, 0], both[:, :, 1])
        send_part = jnp.where(core == 0, both[:, :, 1], both[:, :, 0])
        full = keep_part + lax.ppermute(send_part, "dp", swap)
        hidden = (jax.nn.silu(full[0]) * full[1]).astype(jnp.bfloat16)
        partial = jnp.dot(hidden, hot_w[2], preferred_element_type=jnp.float32)
        by_core = partial.reshape(2, tok_rows, partial.shape[1])
        own_rows = jnp.where(core == 0, by_core[0], by_core[1])
        other_rows = jnp.where(core == 0, by_core[1], by_core[0])
        hot_out = (own_rows + lax.ppermute(other_rows, "dp", swap)).astype(jnp.bfloat16)
        hot_weight = jnp.sum(
            jnp.where(route_ids == hot_id, route_gates, jnp.zeros_like(route_gates)), axis=1
        )
        combined = cold_sum + hot_weight[:, None] * hot_out.astype(jnp.float32)
    return combined.astype(jnp.bfloat16)


def solution(mesh):
    in_specs = (
        P(("expert", "dp"), None),
        P(("expert", "dp"), None, None),
        P(("expert", "dp"), None, None),
        P(("expert", "dp"), None, None),
        P(("expert", "dp"), None),
        P(("expert", "dp"), None),
        P(),
    )
    out_specs = P(("expert", "dp"), None)
    return jax.shard_map(
        on_device, mesh=mesh, in_specs=in_specs, out_specs=out_specs, check_vma=False
    )
```

```python
import functools
import jax
import jax.numpy as jnp
from jax import lax
from jax.sharding import PartitionSpec as P
from jax.experimental import pallas as pl
from jax.experimental.pallas import tpu as pltpu


CAP = 6
MESH = pl.DeviceIdType.MESH


def a2a_kernel(n_dp, x_ref, y_ref, send_sem, recv_sem, local_sem):
    n = x_ref.shape[0]
    me = lax.axis_index("expert") * n_dp + lax.axis_index("dp")

    def peer_copy(src, dst, slot, peer):
        return pltpu.make_async_remote_copy(
            src_ref=x_ref.at[src],
            dst_ref=y_ref.at[dst],
            send_sem=send_sem.at[slot],
            recv_sem=recv_sem.at[slot],
            device_id=(peer // n_dp, peer % n_dp),
            device_id_type=MESH,
        )

    local = pltpu.make_async_copy(x_ref.at[me], y_ref.at[me], local_sem)
    local.start()

    def start(k, carry):
        peer = lax.rem(me + k, n)
        pltpu.make_async_remote_copy(
            src_ref=x_ref.at[peer],
            dst_ref=y_ref.at[me],
            send_sem=send_sem.at[peer],
            recv_sem=recv_sem.at[me],
            device_id=(peer // n_dp, peer % n_dp),
            device_id_type=MESH,
        ).start()
        return carry

    lax.fori_loop(1, n, start, 0)

    def finish(k, carry):
        peer = lax.rem(me + k, n)
        peer_copy(peer, peer, peer, peer).wait_send()
        peer_copy(peer, peer, peer, peer).wait_recv()
        return carry

    lax.fori_loop(1, n, finish, 0)
    local.wait()


def all_to_all_slabs(x, n_dp):
    n = x.shape[0]
    return pl.pallas_call(
        functools.partial(a2a_kernel, n_dp),
        out_shape=jax.ShapeDtypeStruct(x.shape, x.dtype),
        in_specs=[pl.BlockSpec(memory_space=pl.ANY)],
        out_specs=pl.BlockSpec(memory_space=pl.ANY),
        scratch_shapes=[
            pltpu.SemaphoreType.DMA((n,)),
            pltpu.SemaphoreType.DMA((n,)),
            pltpu.SemaphoreType.DMA(()),
        ],
        compiler_params=pltpu.CompilerParams(has_side_effects=True),
    )(x)


def expert_ffn(in_rows, gate_w, up_w, down_w):
    gate_val = jnp.dot(in_rows, gate_w, preferred_element_type=jnp.float32)
    up_val = jnp.dot(in_rows, up_w, preferred_element_type=jnp.float32)
    hidden = (jax.nn.silu(gate_val) * up_val).astype(jnp.bfloat16)
    return jnp.dot(hidden, down_w, preferred_element_type=jnp.float32).astype(jnp.bfloat16)


def on_device(tokens, w_gate, w_up, w_down, route_ids, route_gates, hot_experts):
    tok_rows = tokens.shape[0]
    top_k = route_ids.shape[1]
    n_dp = lax.axis_size("dp")
    experts = lax.axis_size("expert") * n_dp
    hot_id = hot_experts[0]
    me = lax.axis_index("expert") * n_dp + lax.axis_index("dp")
    own = (w_gate[0], w_up[0], w_down[0])

    with jax.named_scope("routing"):
        flat_ids = route_ids.reshape(-1)
        labels = lax.iota(jnp.int32, experts)
        onehot = (flat_ids[:, None] == labels[None, :]).astype(jnp.int32)
        rank_of = jnp.sum(onehot * (jnp.cumsum(onehot, axis=0) - 1), axis=1)
        is_kept = (flat_ids != hot_id) & (rank_of < CAP)
        slot_rank = lax.iota(jnp.int32, CAP)
        hit = (flat_ids[None, None, :] == labels[:, None, None]) & (
            rank_of[None, None, :] == slot_rank[None, :, None]
        ) & is_kept[None, None, :]
        dispatch = jnp.any(hit.reshape(experts, CAP, tok_rows, top_k), axis=3)

    with jax.named_scope("dispatch"):
        outgoing = jnp.einsum(
            "esp,pd->esd", dispatch.astype(tokens.dtype), tokens,
            preferred_element_type=jnp.float32,
        ).astype(tokens.dtype)
        arrived = lax.all_to_all(outgoing, ("expert", "dp"), 0, 0, tiled=True)

    with jax.named_scope("hot_weight_broadcast"):
        core = lax.axis_index("dp")
        partner = me + 1 - 2 * core
        half = own[0].shape[1] // 2
        rows = own[0].shape[0] // 2
        split_g = own[0].reshape(2, rows, own[0].shape[1])
        split_u = own[1].reshape(2, rows, own[1].shape[1])
        split_d = own[2].reshape(2, half, own[2].shape[1])
        mine = (
            jnp.where(core == 0, split_g[0], split_g[1]),
            jnp.where(core == 0, split_u[0], split_u[1]),
            jnp.where(core == 0, split_d[0], split_d[1]),
        )
        theirs = (
            jnp.where(core == 0, split_g[1], split_g[0]),
            jnp.where(core == 0, split_u[1], split_u[0]),
            jnp.where(core == 0, split_d[1], split_d[0]),
        )
        swap = [(0, 1), (1, 0)]
        from_partner = tuple(lax.ppermute(w, "dp", swap) for w in theirs)
        held = tuple(
            jnp.where(me == hot_id, a, jnp.where(partner == hot_id, b, jnp.zeros_like(a)))
            for a, b in zip(mine, from_partner)
        )
        hot_w = tuple(lax.psum(w, "expert") for w in held)

    with jax.named_scope("expert_ffn"):
        results = expert_ffn(arrived.reshape(experts * CAP, -1), *own).reshape(arrived.shape)

    with jax.named_scope("return"):
        returned = lax.all_to_all(results, ("expert", "dp"), 0, 0, tiled=True)

    with jax.named_scope("combine"):
        gate_flat = route_gates.reshape(-1)
        cold_weight = jnp.where(is_kept, gate_flat, jnp.zeros_like(gate_flat))
        weight_of_slot = jnp.where(hit, cold_weight[None, None, :], 0.0)
        combine = jnp.sum(weight_of_slot.reshape(experts, CAP, tok_rows, top_k), axis=3)
        cold_sum = jnp.einsum(
            "esp,esd->pd",
            combine,
            returned.astype(jnp.float32),
            precision=lax.Precision.HIGHEST,
            preferred_element_type=jnp.float32,
        )

    with jax.named_scope("hot_expert"):
        other_tokens = lax.ppermute(tokens, "dp", swap)
        pair = jnp.where(
            core == 0,
            jnp.concatenate([tokens, other_tokens], axis=0),
            jnp.concatenate([other_tokens, tokens], axis=0),
        )
        cold_sum, pair = lax.optimization_barrier((cold_sum, pair))
        cols = pair.reshape(pair.shape[0], 2, rows)
        pair_part = jnp.where(core == 0, cols[:, 0], cols[:, 1])
        gate_part = jnp.dot(pair_part, hot_w[0], preferred_element_type=jnp.float32)
        up_part = jnp.dot(pair_part, hot_w[1], preferred_element_type=jnp.float32)
        both = jnp.stack([gate_part, up_part]).reshape(2, pair.shape[0], 2, half)
        keep_part = jnp.where(core == 0, both[:, :, 0], both[:, :, 1])
        send_part = jnp.where(core == 0, both[:, :, 1], both[:, :, 0])
        full = keep_part + lax.ppermute(send_part, "dp", swap)
        hidden = (jax.nn.silu(full[0]) * full[1]).astype(jnp.bfloat16)
        partial = jnp.dot(hidden, hot_w[2], preferred_element_type=jnp.float32)
        by_core = partial.reshape(2, tok_rows, partial.shape[1])
        own_rows = jnp.where(core == 0, by_core[0], by_core[1])
        other_rows = jnp.where(core == 0, by_core[1], by_core[0])
        other_half = lax.ppermute(other_rows.astype(jnp.bfloat16), "dp", swap)
        hot_out = (own_rows + other_half.astype(jnp.float32)).astype(jnp.bfloat16)
        hot_weight = jnp.sum(
            jnp.where(route_ids == hot_id, route_gates, jnp.zeros_like(route_gates)), axis=1
        )
        combined = cold_sum + hot_weight[:, None] * hot_out.astype(jnp.float32)
    return combined.astype(jnp.bfloat16)


def solution(mesh):
    in_specs = (
        P(("expert", "dp"), None),
        P(("expert", "dp"), None, None),
        P(("expert", "dp"), None, None),
        P(("expert", "dp"), None, None),
        P(("expert", "dp"), None),
        P(("expert", "dp"), None),
        P(),
    )
    out_specs = P(("expert", "dp"), None)
    return jax.shard_map(
        on_device, mesh=mesh, in_specs=in_specs, out_specs=out_specs, check_vma=False
    )
```
